256 devices in a mesh: section: 8 (over y, z_hi), dp: 16 (over z_lo, x), tensor: 2 (over core).
Axes of the slice: x: 4, y: 4, z: 8 (z_hi: 2, z_lo: 4; z = z_hi * 4 + z_lo), core: 2. Of those that a mesh axis runs over, the one named last changes fastest.
Arguments:
- fwd_input: bfloat16 [8, 512, 2048], P('section', 'dp'), may hold values from -40 to 40
- fresh_input: bfloat16 [512, 2048], P('dp'), may hold values from -40 to 40
- cotangent: bfloat16 [8, 512, 2048], P('section', 'dp'), may hold values from -40 to 40
- fresh_cotangent: bfloat16 [512, 2048], P('dp'), may hold values from -40 to 40
- stash: bfloat16 [8, 2, 512, 2048], P('section', None, 'dp'), may hold values from -40 to 40
- norm_gain: float32 [8, 2048], P('section'), may hold values from 0.25 to 1.75
- qk_gain: float32 [8, 2, 128], P('section'), may hold values from 0.25 to 1.75
- w_query: bfloat16 [8, 2048, 2048], P('section', 'dp', 'tensor'), may hold values from -0.125 to 0.125
- w_key: bfloat16 [8, 2048, 256], P('section', 'dp', 'tensor'), may hold values from -0.125 to 0.125
- w_value: bfloat16 [8, 2048, 256], P('section', 'dp', 'tensor'), may hold values from -0.125 to 0.125
- w_out: bfloat16 [8, 2048, 2048], P('section', 'dp', 'tensor'), may hold values from -0.125 to 0.125
Outputs:
- out_activations: bfloat16 [8, 2, 512, 2048], P('section', None, 'dp')
- grad_input: bfloat16 [8, 2, 512, 2048], P('section', None, 'dp')
- grad_query: float32 [8, 2048, 2048], P('section', 'dp', 'tensor')
- grad_key: float32 [8, 2048, 256], P('section', 'dp', 'tensor')
- grad_value: float32 [8, 2048, 256], P('section', 'dp', 'tensor')
- grad_out: float32 [8, 2048, 2048], P('section', 'dp', 'tensor')
- grad_norm_gain: float32 [8, 2048], P('section')
- grad_qk_gain: float32 [8, 2, 128], P('section')
The draws below stay inside these ranges and needn't reach their ends.
All inputs are finite; a program needn't handle non-finite values.
Results may differ from the reference program's by a relative error of at most 0.02.
Values may be sent and summed in bfloat16 or wider, within the bound.
No kernel may reach another device: no remote copies, remote signals or barrier semaphores. Data moves between devices by JAX's collectives and lax.ppermute only.
A program may use at most 64 MiB of HBM per device.

```python
import math
import jax
import jax.numpy as jnp
from jax import lax

D = 2048
HD = 128
HEADS = 16
KV_HEADS = 2
MB = 32
LAYERS = 8
ROWS = 512
WINDOW = 1024
N_DP = 16


def activation_draw(key, shape):
    base = jax.random.truncated_normal(jax.random.fold_in(key, 11), -4.0, 4.0, shape, jnp.float32)
    mixed = base
    return jnp.clip(mixed, -40.0, 40.0).astype(jnp.bfloat16)


def draw_fwd_input(key, part):
    return activation_draw(jax.random.fold_in(key, 101), (LAYERS, ROWS, D))


def draw_fresh_input(key, part):
    return activation_draw(jax.random.fold_in(key, 202), (ROWS, D))


def draw_cotangent(key, part):
    return activation_draw(jax.random.fold_in(key, 303), (LAYERS, ROWS, D))


def draw_fresh_cotangent(key, part):
    return activation_draw(jax.random.fold_in(key, 404), (ROWS, D))


def draw_stash(key, part):
    return activation_draw(jax.random.fold_in(key, 505), (LAYERS, 2, ROWS, D))


def level_of(key, dims, shards, low, largest):
    gain = 1.0
    for position, blocks in shards:
        draws = jax.random.uniform(jax.random.fold_in(jax.random.fold_in(key, 6), position), (blocks,), jnp.float32, low / len(shards), largest / len(shards))
        gain = gain * jnp.repeat(jnp.exp(draws), dims[position] // blocks).reshape((-1,) + (1,) * (len(dims) - 1 - position))
    return gain


def scatter_about(key, extent, deviation, reach, cuts=(), held_as=jnp.bfloat16):
    drawn = deviation * jax.random.normal(key, extent, jnp.float32)
    if cuts:
        drawn = drawn * level_of(key, extent, cuts, -0.22, 0.18)
    return jnp.clip(drawn, -reach, reach).astype(held_as)


def setup_inputs(seed: int = 0) -> dict:
    key_list = jax.random.split(jax.random.key(seed), 12)
    return {
        "fwd_input": draw_fwd_input(jax.random.fold_in(key_list[11], 71), 0),
        "fresh_input": draw_fresh_input(jax.random.fold_in(key_list[11], 71), 0),
        "cotangent": draw_cotangent(jax.random.fold_in(key_list[11], 71), 0),
        "fresh_cotangent": draw_fresh_cotangent(jax.random.fold_in(key_list[11], 71), 0),
        "stash": draw_stash(jax.random.fold_in(key_list[11], 71), 0),
        "norm_gain": jnp.clip(1.0 + 0.15 * jax.random.normal(key_list[5], (LAYERS, D), jnp.float32), 0.25, 1.75),
        "qk_gain": jnp.clip(1.0 + 0.15 * jax.random.normal(key_list[6], (LAYERS, 2, HD), jnp.float32), 0.25, 1.75),
        "w_query": scatter_about(key_list[7], (LAYERS, D, HEADS * HD), D ** -0.5, 0.125, ((0, 8), (1, 16), (2, 2))),
        "w_key": scatter_about(key_list[8], (LAYERS, D, KV_HEADS * HD), D ** -0.5, 0.125, ((0, 8), (1, 16), (2, 2))),
        "w_value": scatter_about(key_list[9], (LAYERS, D, KV_HEADS * HD), D ** -0.5, 0.125, ((0, 8), (1, 16), (2, 2))),
        "w_out": scatter_about(key_list[10], (LAYERS, D, HEADS * HD), (HEADS * HD) ** -0.5, 0.125, ((0, 8), (1, 16), (2, 2))),
    }


EPSILON = 1e-06
THETA = 1000000.0

def rope_tables(length, width):
    half_width = width // 2
    freqs = jnp.exp(jnp.arange(half_width, dtype=jnp.float32) * (-2.0 * math.log(THETA) / width))
    angles = jnp.arange(length, dtype=jnp.float32)[:, None] * freqs[None, :]
    return (jnp.cos(angles), jnp.sin(angles))

def rotate(vectors, cos_tab, sin_tab):
    half_width = vectors.shape[-1] // 2
    first_half = vectors[..., :half_width]
    second_half = vectors[..., half_width:]
    cos_here = cos_tab[:, None, :]
    sin_here = sin_tab[:, None, :]
    return jnp.concatenate([first_half * cos_here - second_half * sin_here, second_half * cos_here + first_half * sin_here], axis=-1)

def head_norm(raw_heads):
    inverse = lax.rsqrt(lax.optimization_barrier(jnp.mean(raw_heads * raw_heads, axis=-1, keepdims=True)) + EPSILON)
    return (raw_heads * inverse, inverse)

def unit_back(grad_unit, unit_row_vectors, inverse):
    return inverse * (grad_unit - unit_row_vectors * lax.optimization_barrier(jnp.mean(grad_unit * unit_row_vectors, axis=-1, keepdims=True)))

def attend_full(normed, w_q, w_k, w_v, qk_gains, cos_tab, sin_tab):
    row_count = normed.shape[0]
    group_size = HEADS // KV_HEADS
    q_unit, q_inv = head_norm(jnp.dot(normed, w_q, preferred_element_type=jnp.float32).reshape(row_count, HEADS, HD))
    k_unit, k_inv = head_norm(jnp.dot(normed, w_k, preferred_element_type=jnp.float32).reshape(row_count, KV_HEADS, HD))
    queries = rotate(q_unit * qk_gains[0], cos_tab, sin_tab).astype(jnp.bfloat16).reshape(row_count, KV_HEADS, group_size, HD)
    keys_b = rotate(k_unit * qk_gains[1], cos_tab, sin_tab).astype(jnp.bfloat16)
    values_b = jnp.dot(normed, w_v, preferred_element_type=jnp.float32).astype(jnp.bfloat16).reshape(row_count, KV_HEADS, HD)
    scores = jnp.einsum('qkgd,tkd->kgqt', queries.astype(jnp.float32), keys_b.astype(jnp.float32)) * (1.0 / math.sqrt(HD))
    causal = lax.broadcasted_iota(jnp.int32, (row_count, row_count), 0) >= lax.broadcasted_iota(jnp.int32, (row_count, row_count), 1)
    expd = jnp.where(causal, jnp.exp(scores), 0.0)
    softmax_f = expd / lax.optimization_barrier(jnp.sum(expd, axis=-1, keepdims=True))
    softmax_b = softmax_f.astype(jnp.bfloat16)
    attended = jnp.einsum('kgqt,tkd->qkgd', softmax_b.astype(jnp.float32), values_b.astype(jnp.float32))
    attended = attended.reshape(row_count, HEADS * HD).astype(jnp.bfloat16)
    return (q_unit, q_inv, k_unit, k_inv, queries, keys_b, values_b, softmax_f, softmax_b, attended)

def input_norm(x_rows, norm_scale):
    x_float = x_rows.astype(jnp.float32)
    inverse = lax.rsqrt(lax.optimization_barrier(jnp.mean(x_float * x_float, axis=-1, keepdims=True)) + EPSILON)
    unit_row_vectors = x_float * inverse
    return (x_float, inverse, unit_row_vectors, (unit_row_vectors * norm_scale).astype(jnp.bfloat16))

def layer_forward(x_rows, norm_scale, w_q, w_k, w_v, w_o, qk_gains, cos_tab, sin_tab):
    x_float, inverse, unit_row_vectors, normed = input_norm(x_rows, norm_scale)
    attended = attend_full(normed, w_q, w_k, w_v, qk_gains, cos_tab, sin_tab)[-1]
    mixed = lax.dot_general(attended, w_o, (((1,), (1,)), ((), ())), preferred_element_type=jnp.float32)
    return (x_float + mixed).astype(jnp.bfloat16)

def layer_backward(x_rows, cot_rows, norm_scale, w_q, w_k, w_v, w_o, qk_gains, cos_tab, sin_tab):
    x_float, inverse, unit_row_vectors, normed = input_norm(x_rows, norm_scale)
    q_unit, q_inv, k_unit, k_inv, queries, keys_b, values_b, softmax_f, softmax_b, attended = attend_full(normed, w_q, w_k, w_v, qk_gains, cos_tab, sin_tab)
    row_count = x_rows.shape[0]
    group_size = HEADS // KV_HEADS
    d_attn = jnp.dot(cot_rows, w_o, preferred_element_type=jnp.float32).astype(jnp.bfloat16).reshape(row_count, KV_HEADS, group_size, HD)
    d_probs = jnp.einsum('qkgd,tkd->kgqt', d_attn.astype(jnp.float32), values_b.astype(jnp.float32))
    d_value = jnp.einsum('kgqt,qkgd->tkd', softmax_b.astype(jnp.float32), d_attn.astype(jnp.float32))
    d_value = d_value.astype(jnp.bfloat16).reshape(row_count, KV_HEADS * HD)
    d_scores = softmax_f * (d_probs - lax.optimization_barrier(jnp.sum(softmax_f * d_probs, axis=-1, keepdims=True))) * (1.0 / math.sqrt(HD))
    d_scores = d_scores.astype(jnp.bfloat16).astype(jnp.float32)
    d_query = jnp.einsum('kgqt,tkd->qkgd', d_scores, keys_b.astype(jnp.float32)).reshape(row_count, HEADS, HD)
    d_key = jnp.einsum('kgqt,qkgd->tkd', d_scores, queries.astype(jnp.float32))
    d_query = rotate(d_query, cos_tab, -sin_tab)
    d_key = rotate(d_key, cos_tab, -sin_tab)
    q_term = lax.optimization_barrier(jnp.sum(d_query * q_unit, axis=(0, 1)))
    k_term = lax.optimization_barrier(jnp.sum(d_key * k_unit, axis=(0, 1)))
    q_grad = unit_back(d_query * qk_gains[0], q_unit, q_inv).astype(jnp.bfloat16).reshape(row_count, HEADS * HD)
    k_grad = unit_back(d_key * qk_gains[1], k_unit, k_inv).astype(jnp.bfloat16).reshape(row_count, KV_HEADS * HD)
    contract = (((1,), (1,)), ((), ()))
    d_normed = lax.dot_general(q_grad, w_q, contract, preferred_element_type=jnp.float32)
    d_normed = d_normed + lax.dot_general(k_grad, w_k, contract, preferred_element_type=jnp.float32)
    d_normed = d_normed + lax.dot_general(d_value, w_v, contract, preferred_element_type=jnp.float32)
    norm_term = lax.optimization_barrier(jnp.sum(d_normed * unit_row_vectors, axis=0))
    d_input = (cot_rows.astype(jnp.float32) + unit_back(d_normed * norm_scale, unit_row_vectors, inverse)).astype(jnp.bfloat16)
    columns = jnp.concatenate([q_grad, k_grad, d_value], axis=1)
    return (d_input, normed, columns, attended, norm_term, q_term, k_term)

def reference(fwd_input, fresh_input, cotangent, fresh_cotangent, stash, norm_gain, qk_gain, w_query, w_key, w_value, w_out):
    cos_tab, sin_tab = rope_tables(MB, HD)
    grad_scale = 1.0 / math.sqrt(WINDOW)

    def as_blocks(array):
        return array.reshape(N_DP, MB, D)

    def forward_section(section_id, blocks_in):

        def apply_one(rows_in):
            return layer_forward(rows_in, norm_gain[section_id], w_query[section_id], w_key[section_id], w_value[section_id], w_out[section_id], qk_gain[section_id], cos_tab, sin_tab)
        return jax.vmap(apply_one)(blocks_in)

    def backward_section(section_id, blocks_in, blocks_cot):

        def apply_one(rows_in, rows_cot):
            return layer_backward(rows_in, rows_cot, norm_gain[section_id], w_query[section_id], w_key[section_id], w_value[section_id], w_out[section_id], qk_gain[section_id], cos_tab, sin_tab)
        return jax.vmap(apply_one)(blocks_in, blocks_cot)
    first_out = [forward_section(section_id, as_blocks(fwd_input[section_id])) for section_id in range(LAYERS)]
    second_in = [as_blocks(fresh_input)] + first_out[:-1]
    second_out = [forward_section(section_id, second_in[section_id]) for section_id in range(LAYERS)]
    mirrored = stash[::-1]
    first_back = [backward_section(section_id, as_blocks(mirrored[section_id, 0]), as_blocks(cotangent[section_id])) for section_id in range(LAYERS)]
    second_cot = [first_back[section_id + 1][0] for section_id in range(LAYERS - 1)] + [as_blocks(fresh_cotangent)]
    second_back = [backward_section(section_id, as_blocks(mirrored[section_id, 1]), second_cot[section_id]) for section_id in range(LAYERS)]
    width_all = 2 * HEADS * HD + 2 * KV_HEADS * HD
    q_width = HEADS * HD
    k_width = KV_HEADS * HD

    def add_block(running, block_items):
        normed_b, cols_b, cots_b, att_b = block_items
        contract = (((0,), (0,)), ((), ()))
        left_term = lax.dot_general(normed_b, cols_b, contract, preferred_element_type=jnp.float32)
        right_term = lax.dot_general(cots_b, att_b, contract, preferred_element_type=jnp.float32)
        partial_b = (jnp.concatenate([left_term, right_term], axis=1) * grad_scale).astype(jnp.bfloat16)
        partial_b = lax.optimization_barrier(partial_b)
        return (running + partial_b.astype(jnp.float32), None)
    grads_q, key_gradients, value_gradients, grads_o, grads_norm, grads_qk = ([], [], [], [], [], [])
    for section_id in range(LAYERS):
        fb = first_back[section_id]
        sb = second_back[section_id]
        normed_rows = jnp.concatenate([fb[1], sb[1]], axis=1)
        col_rows = jnp.concatenate([fb[2], sb[2]], axis=1)
        cot_rows = jnp.concatenate([as_blocks(cotangent[section_id]), second_cot[section_id]], axis=1)
        att_rows = jnp.concatenate([fb[3], sb[3]], axis=1)
        summed, unused = lax.scan(add_block, jnp.zeros((D, width_all), jnp.float32), (normed_rows, col_rows, cot_rows, att_rows))
        grads_q.append(summed[:, :q_width])
        key_gradients.append(summed[:, q_width:q_width + k_width])
        value_gradients.append(summed[:, q_width + k_width:q_width + 2 * k_width])
        grads_o.append(summed[:, q_width + 2 * k_width:])
        grads_norm.append(grad_scale * lax.optimization_barrier(jnp.sum(fb[4] + sb[4], axis=0)))
        grads_qk.append(grad_scale * jnp.stack([lax.optimization_barrier(jnp.sum(fb[5] + sb[5], axis=0)), lax.optimization_barrier(jnp.sum(fb[6] + sb[6], axis=0))]))
    out_activations = jnp.stack([jnp.stack([first_out[section_id], second_out[section_id]]) for section_id in range(LAYERS)]).reshape(LAYERS, 2, ROWS, D)
    grad_input = jnp.stack([jnp.stack([first_back[section_id][0], second_back[section_id][0]]) for section_id in range(LAYERS)]).reshape(LAYERS, 2, ROWS, D)
    return (out_activations, grad_input, jnp.stack(grads_q), jnp.stack(key_gradients), jnp.stack(value_gradients), jnp.stack(grads_o), jnp.stack(grads_norm), jnp.stack(grads_qk))
```

```python
import math

import jax
import jax.numpy as jnp
from jax import lax
from jax.experimental import pallas as pl
from jax.experimental.pallas import tpu as pltpu
from jax.sharding import PartitionSpec as P

HD = 128
EPSILON = 1e-06
THETA = 1000000.0
SIDE = 4
F32 = jnp.float32
BF16 = jnp.bfloat16
INTERPRET = False


LINE_RING = {0: 1, 1: 3, 3: 2, 2: 0}


def z_ring():
    return [(z * SIDE + x, LINE_RING[z] * SIDE + x) for z in range(SIDE) for x in range(SIDE)]


def z_flip(k):
    return [(z * SIDE + x, (z ^ k) * SIDE + x) for z in range(SIDE) for x in range(SIDE)]


def x_shift(by):
    return [(z * SIDE + x, z * SIDE + (x + by) % SIDE) for z in range(SIDE) for x in range(SIDE)]


def x_flip(k):
    return [(z * SIDE + x, z * SIDE + (x ^ k)) for z in range(SIDE) for x in range(SIDE)]


def along_dp(array, route):
    return lax.ppermute(array, "dp", route)


def other_core(array):
    return lax.ppermute(array, "tensor", [(0, 1), (1, 0)])


def gather_weights(shard, z, x):
    rows = shard.shape[0]
    half = rows // 2
    held = [shard]
    for _ in range(SIDE - 1):
        held.append(along_dp(held[-1], z_ring()))
    groups, sources = [], []
    source = z
    for mine in held:
        right = along_dp(mine, x_shift(1))
        left = along_dp(mine, x_shift(-1))
        far_top = along_dp(right[:half], x_shift(1))
        far_low = along_dp(left[half:], x_shift(-1))
        group = jnp.zeros((SIDE * rows, shard.shape[1]), shard.dtype)
        far = (x + 2) % SIDE * rows
        group = lax.dynamic_update_slice(group, mine, (x * rows, 0))
        group = lax.dynamic_update_slice(group, right, ((x + 3) % SIDE * rows, 0))
        group = lax.dynamic_update_slice(group, left, ((x + 1) % SIDE * rows, 0))
        group = lax.dynamic_update_slice(group, far_top, (far, 0))
        group = lax.dynamic_update_slice(group, far_low, (far + half, 0))
        groups.append(group)
        sources.append(source)
        source = jnp.where(source == 0, 2, jnp.where(source == 1, 0, jnp.where(source == 2, 3, 1)))
    return groups, sources


FLIPS = [(j, k) for j in (0, 1, 3, 2) for k in range(SIDE)]


def gather_rows(block):
    mine = jnp.concatenate([block] + [along_dp(block, z_flip(k)) for k in range(1, SIDE)], axis=0)
    half = mine.shape[0] // 2
    near = along_dp(mine, x_flip(1))
    wrap = along_dp(mine, x_flip(3))
    far_top = along_dp(near[:half], x_flip(3))
    far_low = along_dp(wrap[half:], x_flip(1))
    return jnp.concatenate([mine, near, wrap, far_top, far_low], axis=0)


def own_features(blocks, z, x):
    count, rows, features = blocks.shape
    replicas = SIDE * SIDE
    width = features // replicas
    parted = blocks.reshape(count * rows, replicas, width).transpose(1, 0, 2)
    arrived = lax.all_to_all(parted, "dp", 0, 0, tiled=True)
    pieces = [
        lax.dynamic_slice(
            arrived, ((z ^ k) * SIDE + (x ^ j), 0, 0), (1, count * rows, width)
        ).reshape(count, rows, width)
        for j, k in FLIPS
    ]
    return jnp.concatenate(pieces, axis=1)


def sum_over_dp(array):
    for route in (x_flip(1), x_flip(2), z_flip(1), z_flip(2)):
        array = array + along_dp(array, route)
    return array


def stacked(rows_by_columns):
    count = rows_by_columns.shape[1] // HD
    return jnp.concatenate(
        [rows_by_columns[:, i * HD : (i + 1) * HD] for i in range(count)], axis=0
    )


def side_by_side(stack, rows):
    count = stack.shape[0] // rows
    return jnp.concatenate([stack[i * rows : (i + 1) * rows] for i in range(count)], axis=1)


def rope(vectors, cos_tab, sin_tab):
    return vectors * cos_tab + pltpu.roll(vectors, HD // 2, 1) * sin_tab


def unrope(vectors, cos_tab, sin_tab):
    return vectors * cos_tab - pltpu.roll(vectors, HD // 2, 1) * sin_tab


def head_norm(raw):
    inverse = lax.rsqrt(jnp.mean(raw * raw, axis=-1, keepdims=True) + EPSILON)
    return raw * inverse, inverse


def unit_back(grad_unit, unit, inverse):
    return inverse * (grad_unit - unit * jnp.mean(grad_unit * unit, axis=-1, keepdims=True))


def dot(a, b, a_dim, b_dim):
    return lax.dot_general(a, b, (((a_dim,), (b_dim,)), ((), ())), preferred_element_type=F32)


def attend(raw, gains, cos_tab, sin_tab, q_width):
    rows = raw.shape[0]
    q_unit, q_inv = head_norm(stacked(raw[:, :q_width]))
    k_unit, k_inv = head_norm(raw[:, q_width : q_width + HD])
    query = rope(q_unit * gains[0:1], cos_tab, sin_tab).astype(BF16)
    key = rope(k_unit * gains[1:2], cos_tab[:rows], sin_tab[:rows]).astype(BF16)
    value = raw[:, q_width + HD :].astype(BF16)
    scores = dot(query, key, 1, 1) * (1.0 / math.sqrt(HD))
    position = lax.broadcasted_iota(jnp.int32, scores.shape, 0) & (rows - 1)
    causal = position >= lax.broadcasted_iota(jnp.int32, scores.shape, 1)
    raised = jnp.where(causal, jnp.exp(scores), 0.0)
    probs = raised / jnp.sum(raised, axis=-1, keepdims=True)
    probs_b = probs.astype(BF16)
    attn = dot(probs_b, value, 1, 0).astype(BF16)
    return q_unit, q_inv, k_unit, k_inv, query, key, value, probs, probs_b, attn


def forward_kernel(raw_ref, gains_ref, cos_ref, sin_ref, attn_ref):
    rows = 32
    for b in range(raw_ref.shape[0] // rows):
        part = slice(b * rows, (b + 1) * rows)
        attn = attend(
            raw_ref[part, :], gains_ref[...], cos_ref[...], sin_ref[...], attn_ref.shape[1]
        )[-1]
        attn_ref[part, :] = side_by_side(attn, rows)


def backward_kernel(
    raw_ref, d_attn_ref, gains_ref, cos_ref, sin_ref, attn_ref, columns_ref, terms_ref
):
    rows = raw_ref.shape[0]
    gains, cos_tab, sin_tab = gains_ref[...], cos_ref[...], sin_ref[...]
    q_width = attn_ref.shape[1]
    q_unit, q_inv, k_unit, k_inv, query, key, value, probs, probs_b, attn = attend(
        raw_ref[...], gains, cos_tab, sin_tab, q_width
    )
    attn_ref[...] = side_by_side(attn, rows)
    d_attn = stacked(d_attn_ref[...])
    d_probs = dot(d_attn, value, 1, 1)
    d_value = dot(probs_b, d_attn, 0, 0).astype(BF16)
    d_scores = (
        probs
        * (d_probs - jnp.sum(probs * d_probs, axis=-1, keepdims=True))
        * (1.0 / math.sqrt(HD))
    ).astype(BF16)
    dq_r = unrope(dot(d_scores, key, 1, 0), cos_tab, sin_tab)
    dk_r = unrope(dot(d_scores, query, 0, 0), cos_tab[:rows], sin_tab[:rows])
    terms_ref[0:1, :] = jnp.sum(dq_r * q_unit, axis=0, keepdims=True)
    terms_ref[1:2, :] = jnp.sum(dk_r * k_unit, axis=0, keepdims=True)
    q_grad = unit_back(dq_r * gains[0:1], q_unit, q_inv).astype(BF16)
    k_grad = unit_back(dk_r * gains[1:2], k_unit, k_inv).astype(BF16)
    columns_ref[:, :q_width] = side_by_side(q_grad, rows)
    columns_ref[:, q_width : q_width + HD] = k_grad
    columns_ref[:, q_width + HD :] = d_value


def attention_forward(raw, gains, cos_tab, sin_tab, q_width):
    return pl.pallas_call(
        forward_kernel,
        out_shape=jax.ShapeDtypeStruct((raw.shape[0], q_width), BF16),
        interpret=INTERPRET,
    )(raw, gains, cos_tab, sin_tab)


def attention_backward(raw, d_attn, gains, cos_tab, sin_tab):
    return pl.pallas_call(
        backward_kernel,
        out_shape=(
            jax.ShapeDtypeStruct(d_attn.shape, BF16),
            jax.ShapeDtypeStruct(raw.shape, BF16),
            jax.ShapeDtypeStruct((2, HD), F32),
        ),
        interpret=INTERPRET,
    )(raw, d_attn, gains, cos_tab, sin_tab)


def rope_tables(length, copies):
    half_width = HD // 2
    freqs = jnp.exp(jnp.arange(half_width, dtype=F32) * (-2.0 * math.log(THETA) / HD))
    angles = jnp.arange(length, dtype=F32)[:, None] * freqs[None, :]
    cos_half, sin_half = jnp.cos(angles), jnp.sin(angles)
    cos_tab = jnp.concatenate([cos_half, cos_half], axis=1)
    sin_tab = jnp.concatenate([-sin_half, sin_half], axis=1)
    return jnp.tile(cos_tab, (copies, 1)), jnp.tile(sin_tab, (copies, 1))


def input_norm(rows, norm_scale):
    wide = rows.astype(F32)
    inverse = lax.rsqrt(jnp.mean(wide * wide, axis=-1, keepdims=True) + EPSILON)
    unit = wide * inverse
    return inverse, unit, (unit * norm_scale).astype(BF16)


def local(
    fwd_input,
    fresh_input,
    cotangent,
    fresh_cotangent,
    stash,
    norm_gain,
    qk_gain,
    w_query,
    w_key,
    w_value,
    w_out,
):
    replica = lax.axis_index("dp")
    z, x = replica // SIDE, replica % SIDE
    section = lax.axis_index("section")
    sections = lax.axis_size("section")
    core = lax.axis_index("tensor")
    q_width = w_query.shape[2]
    in_width = q_width + w_key.shape[2] + w_value.shape[2]
    rows = fwd_input.shape[1]
    norm_scale, gains = norm_gain[0], qk_gain[0]
    cos_tab, sin_tab = rope_tables(rows, q_width // HD)
    tables = (gains, cos_tab, sin_tab)

    shard = jnp.concatenate([w_query[0], w_key[0], w_value[0], w_out[0]], axis=1)
    groups, sources = gather_weights(shard, z, x)
    mirror = [(s, sections - 1 - s) for s in range(sections)]
    reloaded = lax.ppermute(stash[0], "section", mirror)

    width = groups[0].shape[0]

    def by_rows(activations, first, last):
        total = None
        for group, source in zip(groups, sources):
            part = lax.dynamic_slice(activations, (0, source * width), (activations.shape[0], width))
            product = dot(part, group[:, first:last], 1, 0)
            total = product if total is None else total + product
        return total

    def by_columns(activations, first, last):
        whole = jnp.zeros((activations.shape[0], width * SIDE), BF16)
        for group, source in zip(groups, sources):
            product = dot(activations, group[:, first:last], 1, 1).astype(BF16)
            whole = lax.dynamic_update_slice(whole, product, (0, source * width))
        return whole

    def core_sum(parts):
        parts = lax.optimization_barrier(parts)
        return parts.astype(F32) + other_core(parts).astype(F32)

    def input_grad(cot_rows, d_normed, unit, inverse):
        back = unit_back(d_normed * norm_scale, unit, inverse)
        return (cot_rows.astype(F32) + back).astype(BF16)

    x_first, cot_first = fwd_input[0], cotangent[0]
    inv_1, unit_1, normed_1 = input_norm(reloaded[0], norm_scale)
    inv_2, unit_2, normed_2 = input_norm(reloaded[1], norm_scale)
    normed_f = input_norm(x_first, norm_scale)[2]
    early = own_features(jnp.stack([normed_1, normed_2, cot_first]), z, x)

    raw = by_rows(jnp.concatenate([normed_1, normed_f, normed_2], axis=0), 0, in_width)
    d_attn_1 = by_rows(cot_first, in_width, shard.shape[1]).astype(BF16)
    raw_2 = raw[2 * rows :]
    attn_1, columns_1, terms_1 = attention_backward(raw[:rows], d_attn_1, *tables)
    attn_f2 = attention_forward(raw[rows:], *tables, q_width)
    attn_2 = attn_f2[rows:]
    sums = core_sum(
        jnp.concatenate(
            [
                by_columns(attn_f2[:rows], in_width, shard.shape[1]),
                by_columns(columns_1, 0, in_width),
            ],
            axis=0,
        )
    )
    out_first = (x_first.astype(F32) + sums[:rows]).astype(BF16)
    d_normed_1 = sums[rows:]
    grad_first = input_grad(cot_first, d_normed_1, unit_1, inv_1)

    onward = [(2 * s, 2 * s + 2) for s in range(sections - 1)]
    back = [(2 * s + 1, 2 * s - 1) for s in range(1, sections)]
    passed = lax.ppermute(
        jnp.where(core == 0, out_first, grad_first), ("section", "tensor"), onward + back
    )
    passed = jnp.where((core == 0) & (section == 0), fresh_input, passed)
    passed = jnp.where((core == 1) & (section == sections - 1), fresh_cotangent, passed)
    swapped = other_core(passed)
    x_second = jnp.where(core == 0, passed, swapped)
    cot_second = jnp.where(core == 0, swapped, passed)

    early_rows = gather_rows(jnp.concatenate([columns_1, attn_1, attn_2], axis=1))

    d_attn_2 = by_rows(cot_second, in_width, shard.shape[1]).astype(BF16)
    columns_2, terms_2 = attention_backward(raw_2, d_attn_2, *tables)[1:]
    late_rows = gather_rows(columns_2)
    late = own_features(cot_second[None], z, x)
    raw_f = by_rows(input_norm(x_second, norm_scale)[2], 0, in_width)
    attn_f = attention_forward(raw_f, *tables, q_width)
    sums = core_sum(
        jnp.concatenate(
            [
                by_columns(attn_f, in_width, shard.shape[1]),
                by_columns(columns_2, 0, in_width),
            ],
            axis=0,
        )
    )
    out_second = (x_second.astype(F32) + sums[:rows]).astype(BF16)
    d_normed_2 = sums[rows:]
    grad_second = input_grad(cot_second, d_normed_2, unit_2, inv_2)

    out_activations = jnp.stack([out_first, out_second])[None]
    grad_input = jnp.stack([grad_first, grad_second])[None]

    scale = 1.0 / math.sqrt(2 * rows * lax.axis_size("dp"))
    grad_in = scale * (
        dot(early[0], early_rows[:, :in_width], 0, 0) + dot(early[1], late_rows, 0, 0)
    )
    grad_out = scale * (
        dot(early[2], early_rows[:, in_width : in_width + q_width], 0, 0)
        + dot(late[0], early_rows[:, in_width + q_width :], 0, 0)
    )

    norm_term = jnp.sum(d_normed_1 * unit_1 + d_normed_2 * unit_2, axis=0)
    qk_term = terms_1 + terms_2
    qk_term = qk_term + other_core(qk_term)
    total = sum_over_dp(jnp.concatenate([norm_term.reshape(-1, HD), qk_term], axis=0) * scale)
    return (
        out_activations,
        grad_input,
        grad_in[:, :q_width][None],
        grad_in[:, q_width : q_width + HD][None],
        grad_in[:, q_width + HD :][None],
        grad_out[None],
        total[:-2].reshape(1, -1),
        total[-2:][None],
    )


def solution(mesh):
    return jax.shard_map(
        local,
        mesh=mesh,
        in_specs=(
            P("section", "dp", None),
            P("dp", None),
            P("section", "dp", None),
            P("dp", None),
            P("section", None, "dp", None),
            P("section", None),
            P("section", None, None),
            P("section", "dp", "tensor"),
            P("section", "dp", "tensor"),
            P("section", "dp", "tensor"),
            P("section", "dp", "tensor"),
        ),
        out_specs=(
            P("section", None, "dp", None),
            P("section", None, "dp", None),
            P("section", "dp", "tensor"),
            P("section", "dp", "tensor"),
            P("section", "dp", "tensor"),
            P("section", "dp", "tensor"),
            P("section", None),
            P("section", None, None),
        ),
        check_vma=False,
    )
```

```python
import functools
import math

import jax
import jax.numpy as jnp
from jax import lax
from jax.experimental import pallas as pl
from jax.experimental.pallas import tpu as pltpu
from jax.sharding import PartitionSpec as P


HD = 128
EPSILON = 1e-06
THETA = 1000000.0
SIDE = 4
F32 = jnp.float32
BF16 = jnp.bfloat16
INTERPRET = False
Z_AT, X_AT, CORE_AT = 4, 5, 6
VMEM_LIMIT = 8 * 1024 * 1024


LINE_RING = {0: 1, 1: 3, 3: 2, 2: 0}


def z_ring():
    return [(z * SIDE + x, LINE_RING[z] * SIDE + x) for z in range(SIDE) for x in range(SIDE)]


def z_flip(k):
    return [(z * SIDE + x, (z ^ k) * SIDE + x) for z in range(SIDE) for x in range(SIDE)]


def x_shift(by):
    return [(z * SIDE + x, z * SIDE + (x + by) % SIDE) for z in range(SIDE) for x in range(SIDE)]


def x_flip(k):
    return [(z * SIDE + x, z * SIDE + (x ^ k)) for z in range(SIDE) for x in range(SIDE)]


def along_dp(array, route):
    return lax.ppermute(array, "dp", route)


def other_core(array):
    return lax.ppermute(array, "tensor", [(0, 1), (1, 0)])


def held_until(array, other):
    corner = other[(0,) * (other.ndim - 2)][:16, :HD]
    return lax.optimization_barrier((array, corner))[0]


def gather_weights(shard, z, x):
    rows = shard.shape[0]
    half = rows // 2
    held = [shard]
    for _ in range(1, SIDE):
        held.append(along_dp(held[-1], z_ring()))
    pieces, sources = [], []
    source = z
    far_top = far_low = None
    for step, mine in enumerate(held):
        right = along_dp(mine, x_shift(1))
        left = along_dp(mine, x_shift(-1))
        if step < 2:
            far_top = right[:half]
            far_top = along_dp(far_top, x_shift(1))
        else:
            far_top = along_dp(far_top, z_ring())
        if step < 2:
            far_low = left[half:]
            far_low = along_dp(far_low, x_shift(-1))
        else:
            far_low = along_dp(far_low, z_ring())
        pieces.append((mine, right, left, far_top, far_low))
        sources.append(source)
        source = jnp.where(source == 0, 2, jnp.where(source == 1, 0, jnp.where(source == 2, 3, 1)))
    groups = []
    far = (x + 2) % SIDE * rows
    for step, (mine, right, left, far_top, far_low) in enumerate(pieces):
        if step < 2:
            gate = pieces[2][4]
            far_top, far_low = held_until(far_top, gate), held_until(far_low, gate)
        group = jnp.zeros((SIDE * rows, shard.shape[1]), shard.dtype)
        group = lax.dynamic_update_slice(group, mine, (x * rows, 0))
        group = lax.dynamic_update_slice(group, right, ((x + 3) % SIDE * rows, 0))
        group = lax.dynamic_update_slice(group, left, ((x + 1) % SIDE * rows, 0))
        group = lax.dynamic_update_slice(group, far_top, (far, 0))
        group = lax.dynamic_update_slice(group, far_low, (far + half, 0))
        groups.append(group)
    return groups, jnp.stack(sources)


FLIPS = [(j, k) for j in (0, 1, 3, 2) for k in range(SIDE)]


def gather_rows(block, gate):
    flips = [along_dp(block, z_flip(k)) for k in range(1, SIDE)]
    flips = [held_until(flip, gate) for flip in flips]
    mine = jnp.concatenate([block] + flips, axis=0)
    return mine, *spread_along_x(mine, mine)


def spread_along_x(to_near, to_wrap):
    half = to_near.shape[0] // 2
    near = along_dp(to_near, x_flip(1))
    wrap = along_dp(to_wrap, x_flip(3))
    far_top = along_dp(near[:half], x_flip(3))
    far_low = along_dp(wrap[half:], x_flip(1))
    return near, wrap, far_top, far_low


def own_features(parted):
    width = parted[0].shape[1] // SIDE
    came = [parted[0]]
    came += [along_dp(parted[j], x_flip(j)) for j in range(1, SIDE)]
    stacks = [
        jnp.concatenate([part[:, k * width : (k + 1) * width] for part in came], axis=0)
        for k in range(SIDE)
    ]
    return stacks[:1] + [along_dp(stacks[k], z_flip(k)) for k in range(1, SIDE)]


def sum_over_dp(array):
    for route in (z_flip(1), z_flip(2), x_flip(1), x_flip(2)):
        array = array + along_dp(array, route)
    return array


def stacked(rows_by_columns):
    count = rows_by_columns.shape[1] // HD
    return jnp.concatenate(
        [rows_by_columns[:, i * HD : (i + 1) * HD] for i in range(count)], axis=0
    )


def side_by_side(stack, rows):
    count = stack.shape[0] // rows
    return jnp.concatenate([stack[i * rows : (i + 1) * rows] for i in range(count)], axis=1)


def rope(vectors, cos_tab, sin_tab):
    return vectors * cos_tab + pltpu.roll(vectors, HD // 2, 1) * sin_tab


def unrope(vectors, cos_tab, sin_tab):
    return vectors * cos_tab - pltpu.roll(vectors, HD // 2, 1) * sin_tab


def head_norm(raw):
    inverse = lax.rsqrt(jnp.mean(raw * raw, axis=-1, keepdims=True) + EPSILON)
    return raw * inverse, inverse


def unit_back(grad_unit, unit, inverse):
    return inverse * (grad_unit - unit * jnp.mean(grad_unit * unit, axis=-1, keepdims=True))


def dot(a, b, a_dim, b_dim):
    return lax.dot_general(a, b, (((a_dim,), (b_dim,)), ((), ())), preferred_element_type=F32)


def attend(raw, gains, cos_tab, sin_tab, q_width):
    rows = raw.shape[0]
    q_unit, q_inv = head_norm(stacked(raw[:, :q_width]))
    k_unit, k_inv = head_norm(raw[:, q_width : q_width + HD])
    query = rope(q_unit * gains[0:1], cos_tab, sin_tab).astype(BF16)
    key = rope(k_unit * gains[1:2], cos_tab[:rows], sin_tab[:rows]).astype(BF16)
    value = raw[:, q_width + HD :].astype(BF16)
    scores = dot(query, key, 1, 1) * (1.0 / math.sqrt(HD))
    position = lax.broadcasted_iota(jnp.int32, scores.shape, 0) & (rows - 1)
    causal = position >= lax.broadcasted_iota(jnp.int32, scores.shape, 1)
    raised = jnp.where(causal, jnp.exp(scores), 0.0)
    probs = raised / jnp.sum(raised, axis=-1, keepdims=True)
    probs_b = probs.astype(BF16)
    attn = dot(probs_b, value, 1, 0).astype(BF16)
    return q_unit, q_inv, k_unit, k_inv, query, key, value, probs, probs_b, attn


def columns_of(activations, groups, src_ref, out_ref, top, first, last):
    rows = activations.shape[0]
    for i, group in enumerate(groups):
        width = group.shape[0]
        at = pl.multiple_of(src_ref[i] * width, width)
        product = dot(activations, group[:, first:last], 1, 1).astype(BF16)
        out_ref[top : top + rows, pl.ds(at, width)] = product


def rows_of(read, groups, src_ref, first, last):
    total = None
    for i, group in enumerate(groups):
        width = group.shape[0]
        part = read(pl.ds(pl.multiple_of(src_ref[i] * width, width), width))
        product = dot(part, group[:, first:last], 1, 0)
        total = product if total is None else total + product
    return total


def back_attention(raw, d_attn, gains, cos_tab, sin_tab, terms_ref):
    rows = raw.shape[0]
    q_unit, q_inv, k_unit, k_inv, query, key, value, probs, probs_b, attn = attend(
        raw, gains, cos_tab, sin_tab, d_attn.shape[1]
    )
    d_attn = stacked(d_attn)
    d_probs = dot(d_attn, value, 1, 1)
    d_value = dot(probs_b, d_attn, 0, 0).astype(BF16)
    d_scores = (
        probs
        * (d_probs - jnp.sum(probs * d_probs, axis=-1, keepdims=True))
        * (1.0 / math.sqrt(HD))
    ).astype(BF16)
    dq_r = unrope(dot(d_scores, key, 1, 0), cos_tab, sin_tab)
    dk_r = unrope(dot(d_scores, query, 0, 0), cos_tab[:rows], sin_tab[:rows])
    terms_ref[0:1, :] = jnp.sum(dq_r * q_unit, axis=0, keepdims=True)
    terms_ref[1:2, :] = jnp.sum(dk_r * k_unit, axis=0, keepdims=True)
    q_grad = unit_back(dq_r * gains[0:1], q_unit, q_inv).astype(BF16)
    k_grad = unit_back(dk_r * gains[1:2], k_unit, k_inv).astype(BF16)
    columns = jnp.concatenate([side_by_side(q_grad, rows), k_grad, d_value], axis=1)
    return side_by_side(attn, rows), columns


def first_kernel(
    src_ref, raw_ref, d_attn_ref, gains_ref, cos_ref, sin_ref, g0, g1, g2, g3,
    parts_ref, early_ref, terms_ref,
):
    rows, q_width = d_attn_ref.shape
    in_width = raw_ref.shape[1]
    groups = (g0, g1, g2, g3)
    tables = (gains_ref[...], cos_ref[...], sin_ref[...])
    attn_1, columns = back_attention(
        raw_ref[:rows, :], d_attn_ref[...].astype(BF16), *tables, terms_ref
    )
    attn_f = side_by_side(attend(raw_ref[rows : 2 * rows, :], *tables, q_width)[-1], rows)
    attn_2 = side_by_side(attend(raw_ref[2 * rows :, :], *tables, q_width)[-1], rows)
    early_ref[:, :in_width] = columns
    early_ref[:, in_width : in_width + q_width] = attn_1
    early_ref[:, in_width + q_width :] = attn_2
    columns_of(attn_f, groups, src_ref, parts_ref, 0, in_width, in_width + q_width)
    columns_of(columns, groups, src_ref, parts_ref, rows, 0, in_width)


def prepare_kernel(
    info_ref, first_ref, second_ref, x_ref, cot_ref, scale_ref, normed_ref, p0, p1, p2, p3
):
    rows, features = cot_ref.shape
    for i, saved in enumerate((first_ref, x_ref, second_ref)):
        normed_ref[i * rows : (i + 1) * rows, :] = input_norm(saved[...], scale_ref[...])[2]
    width = features // (SIDE * SIDE)
    for j, part in enumerate((p0, p1, p2, p3)):
        for k in range(SIDE):
            replica = (info_ref[Z_AT] ^ k) * SIDE + (info_ref[X_AT] ^ j)
            here = pl.ds(pl.multiple_of(replica * width, width), width)
            at = 3 * k * width
            part[:, at : at + width] = normed_ref[0:rows, here]
            part[:, at + width : at + 2 * width] = normed_ref[2 * rows : 3 * rows, here]
            part[:, at + 2 * width : at + 3 * width] = cot_ref[:, here]


def backward_kernel(
    src_ref, raw_ref, cot_ref, gains_ref, cos_ref, sin_ref, g0, g1, g2, g3,
    c0, c1, c2, c3, part_ref, terms_ref,
):
    rows, features = cot_ref.shape
    in_width = raw_ref.shape[1]
    groups = (g0, g1, g2, g3)
    d_attn = rows_of(lambda at: cot_ref[:, at], groups, src_ref, in_width, g0.shape[1])
    columns = back_attention(
        raw_ref[2 * rows :, :], d_attn.astype(BF16), gains_ref[...], cos_ref[...], sin_ref[...],
        terms_ref,
    )[1]
    width = features // SIDE
    for k, payload in enumerate((c0, c1, c2, c3)):
        payload[:, :in_width] = columns
        at = pl.multiple_of((src_ref[Z_AT] ^ k) * width, width)
        payload[:, in_width:] = cot_ref[:, pl.ds(at, width)]
    columns_of(columns, groups, src_ref, part_ref, 0, 0, in_width)


def spread_kernel(info_ref, c0, c1, c2, c3, mine_ref, near_ref, wrap_ref):
    rows = c0.shape[0]
    in_width = mine_ref.shape[1] - HD
    for k, part in enumerate((c0, c1, c2, c3)):
        here = slice(k * rows, (k + 1) * rows)
        for out_ref, flips in ((mine_ref, (0,)), (near_ref, (1, 2)), (wrap_ref, (3, 2))):
            out_ref[here, :in_width] = part[:, :in_width]
            for i, j in enumerate(flips):
                at = pl.multiple_of(in_width + (info_ref[X_AT] ^ j) * HD, HD)
                to = in_width + i * HD
                out_ref[here, to : to + HD] = part[:, pl.ds(at, HD)]


def forward_kernel(
    src_ref, x_ref, scale_ref, gains_ref, cos_ref, sin_ref, g0, g1, g2, g3, part_ref, normed_ref
):
    rows = x_ref.shape[0]
    total = g0.shape[1]
    q_width = HD * (cos_ref.shape[0] // rows)
    in_width = total - q_width
    groups = (g0, g1, g2, g3)
    normed_ref[...] = input_norm(x_ref[...], scale_ref[...])[2]
    raw = rows_of(lambda at: normed_ref[:, at], groups, src_ref, 0, in_width)
    attn = attend(raw, gains_ref[...], cos_ref[...], sin_ref[...], q_width)[-1]
    columns_of(side_by_side(attn, rows), groups, src_ref, part_ref, 0, in_width, total)


def post_kernel(
    core_ref, own_ref, other_ref, x_ref, cot_ref, saved_ref, scale_ref,
    out_ref, grad_ref, passed_ref, norm_ref,
):
    rows = x_ref.shape[0]
    sums = own_ref[...].astype(F32) + other_ref[...].astype(F32)
    out = (x_ref[...].astype(F32) + sums[:rows]).astype(BF16)
    inverse, unit, _ = input_norm(saved_ref[...], scale_ref[...])
    d_normed = sums[rows:]
    back = unit_back(d_normed * scale_ref[...], unit, inverse)
    grad = (cot_ref[...].astype(F32) + back).astype(BF16)
    out_ref[...] = out
    grad_ref[...] = grad
    norm_ref[...] = jnp.sum(d_normed * unit, axis=0, keepdims=True)

    @pl.when(core_ref[CORE_AT] == 0)
    def _():
        passed_ref[...] = out

    @pl.when(core_ref[CORE_AT] != 0)
    def _():
        passed_ref[...] = grad


def weights_kernel(
    info_ref, n0, n1, n2, n3, e0, e1, e2, e3, e4, l0, l1, l2, l3, l4,
    query_ref, key_ref, value_ref, out_ref, features_ref, *, scale
):
    rows = n0.shape[0] // SIDE
    q_width = query_ref.shape[2]
    in_width = q_width + 2 * HD
    for i, (j, k) in enumerate(FLIPS):
        for c in range(3):
            features_ref[c, i * rows : (i + 1) * rows, :] = (n0, n1, n2, n3)[k][
                j * rows : (j + 1) * rows, c * HD : (c + 1) * HD
            ]
    grad_in, grad_out, at = 0.0, 0.0, 0
    for i, (early, late) in enumerate(zip((e0, e1, e2, e3, e4), (l0, l1, l2, l3, l4))):
        here = slice(at, at + early.shape[0])
        at += early.shape[0]
        cot_at = in_width + (HD if i > 2 else 0)
        grad_in += dot(features_ref[0, here, :], early[:, :in_width], 0, 0)
        grad_in += dot(features_ref[1, here, :], late[:, :in_width], 0, 0)
        grad_out += dot(features_ref[2, here, :], early[:, in_width : in_width + q_width], 0, 0)
        grad_out += dot(late[:, cot_at : cot_at + HD], early[:, in_width + q_width :], 0, 0)
    query_ref[0] = scale * grad_in[:, :q_width]
    key_ref[0] = scale * grad_in[:, q_width : q_width + HD]
    value_ref[0] = scale * grad_in[:, q_width + HD :]
    out_ref[0] = scale * grad_out


def kernel_call(kernel, out_shape, *operands, scratch=()):
    spec = [pl.BlockSpec(memory_space=pltpu.SMEM)]
    spec += [pl.BlockSpec(memory_space=pltpu.VMEM)] * (len(operands) - 1)
    return pl.pallas_call(
        kernel,
        in_specs=spec,
        out_specs=jax.tree.map(lambda _: pl.BlockSpec(memory_space=pltpu.VMEM), out_shape),
        out_shape=out_shape,
        scratch_shapes=scratch,
        compiler_params=pltpu.CompilerParams(vmem_limit_bytes=VMEM_LIMIT),
        interpret=INTERPRET,
    )(*operands)


def rope_tables(length, copies):
    half_width = HD // 2
    freqs = jnp.exp(jnp.arange(half_width, dtype=F32) * (-2.0 * math.log(THETA) / HD))
    angles = jnp.arange(length, dtype=F32)[:, None] * freqs[None, :]
    cos_half, sin_half = jnp.cos(angles), jnp.sin(angles)
    cos_tab = jnp.concatenate([cos_half, cos_half], axis=1)
    sin_tab = jnp.concatenate([-sin_half, sin_half], axis=1)
    return jnp.tile(cos_tab, (copies, 1)), jnp.tile(sin_tab, (copies, 1))


def input_norm(rows, norm_scale):
    wide = rows.astype(F32)
    inverse = lax.rsqrt(jnp.mean(wide * wide, axis=-1, keepdims=True) + EPSILON)
    unit = wide * inverse
    return inverse, unit, (unit * norm_scale).astype(BF16)


def local(
    fwd_input,
    fresh_input,
    cotangent,
    fresh_cotangent,
    stash,
    norm_gain,
    qk_gain,
    w_query,
    w_key,
    w_value,
    w_out,
):
    replica = lax.axis_index("dp")
    z, x = replica // SIDE, replica % SIDE
    section = lax.axis_index("section")
    sections = lax.axis_size("section")
    core = lax.axis_index("tensor")
    q_width = w_query.shape[2]
    in_width = q_width + w_key.shape[2] + w_value.shape[2]
    rows = fwd_input.shape[1]
    norm_scale, gains = norm_gain[0], qk_gain[0]
    cos_tab, sin_tab = rope_tables(rows, q_width // HD)
    tables = (gains, cos_tab, sin_tab)

    shard = jnp.concatenate([w_query[0], w_key[0], w_value[0], w_out[0]], axis=1)
    total_width = shard.shape[1]
    groups, sources = gather_weights(shard, z, x)
    info = jnp.concatenate([sources, jnp.stack([z, x, core])])
    mirror = [(s, sections - 1 - s) for s in range(sections)]
    fetched = lax.ppermute(jnp.where(core == 0, stash[0, 0], stash[0, 1]), "section", mirror)
    shared = other_core(fetched)
    reloaded = jnp.where(core == 0, fetched, shared), jnp.where(core == 0, shared, fetched)
    width = groups[0].shape[0]
    features = width * SIDE

    def by_rows(activations, first, last):
        total = None
        for i, group in enumerate(groups):
            part = lax.dynamic_slice(
                activations, (0, sources[i] * width), (activations.shape[0], width)
            )
            product = dot(part, group[:, first:last], 1, 0)
            total = product if total is None else total + product
        return total

    def core_sum(parts):
        parts = lax.optimization_barrier(parts)
        return parts.astype(F32) + other_core(parts).astype(F32)

    def input_grad(cot_rows, d_normed, unit, inverse):
        back = unit_back(d_normed * norm_scale, unit, inverse)
        return (cot_rows.astype(F32) + back).astype(BF16)

    x_first, cot_first = fwd_input[0], cotangent[0]
    inv_2, unit_2, _ = input_norm(reloaded[1], norm_scale)
    parted = jax.ShapeDtypeStruct((rows, 3 * features // SIDE), BF16)
    normed, *parted = kernel_call(
        prepare_kernel,
        (jax.ShapeDtypeStruct((3 * rows, features), BF16), parted, parted, parted, parted),
        info, *reloaded, x_first, cot_first, norm_gain,
    )
    early = own_features(parted)
    raw = by_rows(normed, 0, in_width)
    d_attn_1 = by_rows(cot_first, in_width, total_width)
    parts, early_block, terms_1 = kernel_call(
        first_kernel,
        (
            jax.ShapeDtypeStruct((2 * rows, features), BF16),
            jax.ShapeDtypeStruct((rows, in_width + 2 * q_width), BF16),
            jax.ShapeDtypeStruct((2, HD), F32),
        ),
        info, raw, d_attn_1, *tables, *groups,
    )
    block = jax.ShapeDtypeStruct((rows, features), BF16)
    out_first, grad_first, passed, norm_term_1 = kernel_call(
        post_kernel,
        (block, block, block, jax.ShapeDtypeStruct((1, features), F32)),
        info, parts, other_core(parts),
        x_first, cot_first, reloaded[0], norm_gain,
    )

    onward = [(2 * s, 2 * s + 2) for s in range(sections - 1)]
    back = [(2 * s + 1, 2 * s - 1) for s in range(1, sections)]
    passed = lax.ppermute(passed, ("section", "tensor"), onward + back)
    passed = jnp.where((core == 0) & (section == 0), fresh_input, passed)
    passed = jnp.where((core == 1) & (section == sections - 1), fresh_cotangent, passed)
    swapped = other_core(passed)
    x_second = jnp.where(core == 0, passed, swapped)
    cot_second = jnp.where(core == 0, swapped, passed)

    early_rows = gather_rows(early_block, passed)

    payload = jax.ShapeDtypeStruct((rows, in_width + width), BF16)
    *payloads, back_part, terms_2 = kernel_call(
        backward_kernel,
        (payload, payload, payload, payload, block, jax.ShapeDtypeStruct((2, HD), F32)),
        info, raw, cot_second, *tables, *groups,
    )
    out_part = kernel_call(
        forward_kernel,
        jax.ShapeDtypeStruct((rows, features), BF16),
        info, x_second, norm_gain, *tables, *groups,
        scratch=[pltpu.VMEM((rows, features), BF16)],
    )
    d_normed_2 = core_sum(back_part)
    grad_second = input_grad(cot_second, d_normed_2, unit_2, inv_2)
    other_part = other_core(out_part)
    out_sum = out_part.astype(F32) + other_part.astype(F32)
    out_second = (x_second.astype(F32) + out_sum).astype(BF16)
    flips = [along_dp(payloads[k], z_flip(k)) for k in range(1, SIDE)]
    flips = [held_until(flip, other_part) for flip in flips]
    onto_x = jax.ShapeDtypeStruct((SIDE * rows, in_width + 2 * HD), BF16)
    mine, to_near, to_wrap = kernel_call(
        spread_kernel,
        (jax.ShapeDtypeStruct((SIDE * rows, in_width + HD), BF16), onto_x, onto_x),
        info, payloads[0], *flips,
    )
    late_rows = mine, *spread_along_x(to_near, to_wrap)

    out_activations = jnp.stack([out_first, out_second])[None]
    grad_input = jnp.stack([grad_first, grad_second])[None]

    scale = 1.0 / math.sqrt(2 * rows * lax.axis_size("dp"))
    like = [jax.ShapeDtypeStruct(w.shape, F32) for w in (w_query, w_key, w_value, w_out)]
    grads = kernel_call(
        functools.partial(weights_kernel, scale=scale),
        tuple(like),
        info, *early, *early_rows, *late_rows,
        scratch=[pltpu.VMEM((3, rows * SIDE * SIDE, HD), BF16)],
    )

    norm_term = norm_term_1[0] + jnp.sum(d_normed_2 * unit_2, axis=0)
    qk_term = terms_1 + terms_2
    qk_term = qk_term + other_core(qk_term)
    total = sum_over_dp(jnp.concatenate([norm_term.reshape(-1, HD), qk_term], axis=0) * scale)
    return (
        out_activations,
        grad_input,
        *grads,
        total[:-2].reshape(1, -1),
        total[-2:][None],
    )


def solution(mesh):
    return jax.shard_map(
        local,
        mesh=mesh,
        in_specs=(
            P("section", "dp", None),
            P("dp", None),
            P("section", "dp", None),
            P("dp", None),
            P("section", None, "dp", None),
            P("section", None),
            P("section", None, None),
            P("section", "dp", "tensor"),
            P("section", "dp", "tensor"),
            P("section", "dp", "tensor"),
            P("section", "dp", "tensor"),
        ),
        out_specs=(
            P("section", None, "dp", None),
            P("section", None, "dp", None),
            P("section", "dp", "tensor"),
            P("section", "dp", "tensor"),
            P("section", "dp", "tensor"),
            P("section", "dp", "tensor"),
            P("section", None),
            P("section", None, None),
        ),
        check_vma=False,
    )
```

```python
import functools
import math

import jax
import jax.numpy as jnp
from jax import lax
from jax.experimental import pallas as pl
from jax.experimental.pallas import tpu as pltpu
from jax.sharding import PartitionSpec as P


HD = 128
EPSILON = 1e-06
THETA = 1000000.0
SIDE = 4
F32 = jnp.float32
BF16 = jnp.bfloat16
INTERPRET = False
Z_AT, X_AT, CORE_AT = 4, 5, 6
VMEM_LIMIT = 16 * 1024 * 1024


LINE_RING = {0: 1, 1: 3, 3: 2, 2: 0}


def z_ring():
    return [(z * SIDE + x, LINE_RING[z] * SIDE + x) for z in range(SIDE) for x in range(SIDE)]


def z_flip(k):
    return [(z * SIDE + x, (z ^ k) * SIDE + x) for z in range(SIDE) for x in range(SIDE)]


def x_flip(k):
    return [(z * SIDE + x, z * SIDE + (x ^ k)) for z in range(SIDE) for x in range(SIDE)]


def along_dp(array, route):
    return lax.ppermute(array, "dp", route)


def other_core(array):
    return lax.ppermute(array, "tensor", [(0, 1), (1, 0)])


def held_until(array, other):
    corner = other[(0,) * (other.ndim - 2)][:16, :HD]
    return lax.optimization_barrier((array, corner))[0]


def gather_weights(shard, z):
    rows = shard.shape[0]
    half = rows // 2
    held = [shard]
    for _ in range(1, SIDE):
        held.append(along_dp(held[-1], z_ring()))
    pieces, sources = [], []
    source = z
    for step, mine in enumerate(held):
        near = along_dp(mine, x_flip(1))
        wrap = along_dp(mine, x_flip(3))
        if step < 2:
            far_top = near[:half]
            far_low = wrap[half:]
            far_top = along_dp(far_top, x_flip(3))
            far_low = along_dp(far_low, x_flip(1))
            across = far_top, far_low
            if step == 1:
                across = (jnp.concatenate(across, axis=0),)
        else:
            across = (along_dp(across[0], z_ring()),)
        pieces.append((mine, near, wrap, *across))
        sources.append(source)
        source = jnp.where(source == 0, 2, jnp.where(source == 1, 0, jnp.where(source == 2, 3, 1)))
    return pieces, jnp.stack(sources)


FLIPS = [(j, k) for j in (0, 1, 3, 2) for k in range(SIDE)]


def gather_rows(block, gate):
    flips = [along_dp(block, z_flip(k)) for k in range(1, SIDE)]
    flips = [held_until(flip, gate) for flip in flips]
    mine = jnp.concatenate([block] + flips, axis=0)
    return mine, *spread_along_x(mine, mine)


def spread_along_x(to_near, to_wrap):
    half = to_near.shape[0] // 2
    near = along_dp(to_near, x_flip(1))
    wrap = along_dp(to_wrap, x_flip(3))
    far_top = along_dp(near[:half], x_flip(3))
    far_low = along_dp(wrap[half:], x_flip(1))
    return near, wrap, far_top, far_low


def sent_along_x(parted):
    flips = [along_dp(parted[j], x_flip(j)) for j in range(1, SIDE)]
    return parted[:1] + flips


def own_features(came):
    width = came[0].shape[1] // SIDE
    stacks = [
        jnp.concatenate([part[:, k * width : (k + 1) * width] for part in came], axis=0)
        for k in range(SIDE)
    ]
    return stacks[:1] + [along_dp(stacks[k], z_flip(k)) for k in range(1, SIDE)]


def sum_over_dp(array):
    for route in (x_flip(1), x_flip(2), z_flip(1), z_flip(2)):
        array = array + along_dp(array, route)
    return array


def stacked(rows_by_columns):
    count = rows_by_columns.shape[1] // HD
    return jnp.concatenate(
        [rows_by_columns[:, i * HD : (i + 1) * HD] for i in range(count)], axis=0
    )


def side_by_side(stack, rows):
    count = stack.shape[0] // rows
    return jnp.concatenate([stack[i * rows : (i + 1) * rows] for i in range(count)], axis=1)


def rope(vectors, cos_tab, sin_tab):
    return vectors * cos_tab + pltpu.roll(vectors, HD // 2, 1) * sin_tab


def unrope(vectors, cos_tab, sin_tab):
    return vectors * cos_tab - pltpu.roll(vectors, HD // 2, 1) * sin_tab


def head_norm(raw):
    inverse = lax.rsqrt(jnp.mean(raw * raw, axis=-1, keepdims=True) + EPSILON)
    return raw * inverse, inverse


def unit_back(grad_unit, unit, inverse):
    return inverse * (grad_unit - unit * jnp.mean(grad_unit * unit, axis=-1, keepdims=True))


def dot(a, b, a_dim, b_dim):
    return lax.dot_general(a, b, (((a_dim,), (b_dim,)), ((), ())), preferred_element_type=F32)


def attend(raw, gains, cos_tab, sin_tab, q_width):
    rows = raw.shape[0]
    q_unit, q_inv = head_norm(stacked(raw[:, :q_width]))
    k_unit, k_inv = head_norm(raw[:, q_width : q_width + HD])
    query = rope(q_unit * gains[0:1], cos_tab, sin_tab).astype(BF16)
    key = rope(k_unit * gains[1:2], cos_tab[:rows], sin_tab[:rows]).astype(BF16)
    value = raw[:, q_width + HD :].astype(BF16)
    scores = dot(query, key, 1, 1) * (1.0 / math.sqrt(HD))
    position = lax.broadcasted_iota(jnp.int32, scores.shape, 0) & (rows - 1)
    causal = position >= lax.broadcasted_iota(jnp.int32, scores.shape, 1)
    raised = jnp.where(causal, jnp.exp(scores), 0.0)
    probs = raised / jnp.sum(raised, axis=-1, keepdims=True)
    probs_b = probs.astype(BF16)
    attn = dot(probs_b, value, 1, 0).astype(BF16)
    return q_unit, q_inv, k_unit, k_inv, query, key, value, probs, probs_b, attn


def columns_of(activations, weights_ref, src_ref, out_ref, top, first, last):
    rows = activations.shape[0]
    width = out_ref.shape[1] // SIDE

    def group(i, carry):
        at = pl.multiple_of(src_ref[i] * width, width)
        here = pl.ds(pl.multiple_of(i * width, width), width)
        product = dot(activations, weights_ref[here, first:last], 1, 1).astype(BF16)
        out_ref[top : top + rows, pl.ds(at, width)] = product
        return carry

    lax.fori_loop(0, SIDE, group, 0)


def rows_of(rows_ref, weights_ref, src_ref, sum_ref, first, last):
    width = rows_ref.shape[1] // SIDE
    sum_ref[...] = jnp.zeros(sum_ref.shape, F32)

    def group(i, carry):
        at = pl.multiple_of(src_ref[i] * width, width)
        here = pl.ds(pl.multiple_of(i * width, width), width)
        sum_ref[...] += dot(rows_ref[:, pl.ds(at, width)], weights_ref[here, first:last], 1, 0)
        return carry

    lax.fori_loop(0, SIDE, group, 0)


def back_attention(raw, d_attn, gains, cos_tab, sin_tab, terms_ref):
    rows = raw.shape[0]
    q_unit, q_inv, k_unit, k_inv, query, key, value, probs, probs_b, attn = attend(
        raw, gains, cos_tab, sin_tab, d_attn.shape[1]
    )
    d_attn = stacked(d_attn)
    d_probs = dot(d_attn, value, 1, 1)
    d_value = dot(probs_b, d_attn, 0, 0).astype(BF16)
    d_scores = (
        probs
        * (d_probs - jnp.sum(probs * d_probs, axis=-1, keepdims=True))
        * (1.0 / math.sqrt(HD))
    ).astype(BF16)
    dq_r = unrope(dot(d_scores, key, 1, 0), cos_tab, sin_tab)
    dk_r = unrope(dot(d_scores, query, 0, 0), cos_tab[:rows], sin_tab[:rows])
    terms_ref[0:1, :] = jnp.sum(dq_r * q_unit, axis=0, keepdims=True)
    terms_ref[1:2, :] = jnp.sum(dk_r * k_unit, axis=0, keepdims=True)
    q_grad = unit_back(dq_r * gains[0:1], q_unit, q_inv).astype(BF16)
    k_grad = unit_back(dk_r * gains[1:2], k_unit, k_inv).astype(BF16)
    columns = jnp.concatenate([side_by_side(q_grad, rows), k_grad, d_value], axis=1)
    return side_by_side(attn, rows), columns


TILE = 16


def put_group(step, pieces, src_ref, weights_ref):
    size = pieces[0].shape[0]
    places = [(0, 0), (1, 0), (3, 0), (2, 0), (2, pieces[3].shape[0])]
    for piece, (flip, down) in zip(pieces, places):
        top = (step * SIDE + (src_ref[X_AT] ^ flip)) * size + down

        def put(i, carry, piece=piece, top=top):
            here = pl.multiple_of(i * TILE, TILE)
            there = pl.multiple_of(top + i * TILE, TILE)
            weights_ref[pl.ds(there, TILE), :] = piece[pl.ds(here, TILE), :]
            return carry

        lax.fori_loop(0, piece.shape[0] // TILE, put, 0)


def three_groups_kernel(src_ref, *refs):
    *pieces, weights_ref = refs
    put_group(0, pieces[:5], src_ref, weights_ref)
    put_group(1, pieces[5:9], src_ref, weights_ref)
    put_group(2, pieces[9:13], src_ref, weights_ref)


def first_kernel(
    src_ref, normed_ref, cot_ref, gains_ref, cos_ref, sin_ref, s0, s1, s2, s3, three_ref,
    parts_ref, early_ref, terms_ref, raw_2_ref, weights_ref, raw_ref, d_attn_ref,
):
    put_group(3, (s0, s1, s2, s3), src_ref, weights_ref)
    rows, q_width = d_attn_ref.shape
    in_width = raw_ref.shape[1]
    total = weights_ref.shape[1]
    rows_of(normed_ref, weights_ref, src_ref, raw_ref, 0, in_width)
    rows_of(cot_ref, weights_ref, src_ref, d_attn_ref, in_width, total)
    raw_2_ref[...] = raw_ref[2 * rows :, :]
    tables = (gains_ref[...], cos_ref[...], sin_ref[...])
    attn_1, columns = back_attention(
        raw_ref[:rows, :], d_attn_ref[...].astype(BF16), *tables, terms_ref
    )
    attn_f = side_by_side(attend(raw_ref[rows : 2 * rows, :], *tables, q_width)[-1], rows)
    attn_2 = side_by_side(attend(raw_ref[2 * rows :, :], *tables, q_width)[-1], rows)
    early_ref[:, :in_width] = columns
    early_ref[:, in_width : in_width + q_width] = attn_1
    early_ref[:, in_width + q_width :] = attn_2
    columns_of(attn_f, weights_ref, src_ref, parts_ref, 0, in_width, total)
    columns_of(columns, weights_ref, src_ref, parts_ref, rows, 0, in_width)


def prepare_kernel(
    info_ref, first_ref, second_ref, x_ref, cot_ref, scale_ref, normed_ref, p0, p1, p2, p3
):
    rows, features = cot_ref.shape
    for i, saved in enumerate((first_ref, x_ref, second_ref)):
        normed_ref[i * rows : (i + 1) * rows, :] = input_norm(saved[...], scale_ref[...])[2]
    width = features // (SIDE * SIDE)
    for j, part in enumerate((p0, p1, p2, p3)):
        for k in range(SIDE):
            replica = (info_ref[Z_AT] ^ k) * SIDE + (info_ref[X_AT] ^ j)
            here = pl.ds(pl.multiple_of(replica * width, width), width)
            at = 3 * k * width
            part[:, at : at + width] = normed_ref[0:rows, here]
            part[:, at + width : at + 2 * width] = normed_ref[2 * rows : 3 * rows, here]
            part[:, at + 2 * width : at + 3 * width] = cot_ref[:, here]


def backward_kernel(
    src_ref, raw_ref, cot_ref, gains_ref, cos_ref, sin_ref, weights_ref,
    c0, c1, c2, c3, part_ref, terms_ref, d_attn_ref,
):
    features = cot_ref.shape[1]
    in_width = raw_ref.shape[1]
    rows_of(cot_ref, weights_ref, src_ref, d_attn_ref, in_width, weights_ref.shape[1])
    columns = back_attention(
        raw_ref[...], d_attn_ref[...].astype(BF16), gains_ref[...], cos_ref[...], sin_ref[...],
        terms_ref,
    )[1]
    width = features // SIDE
    for k, payload in enumerate((c0, c1, c2, c3)):
        payload[:, :in_width] = columns
        at = pl.multiple_of((src_ref[Z_AT] ^ k) * width, width)
        payload[:, in_width:] = cot_ref[:, pl.ds(at, width)]
    columns_of(columns, weights_ref, src_ref, part_ref, 0, 0, in_width)


def spread_kernel(info_ref, c0, c1, c2, c3, mine_ref, near_ref, wrap_ref):
    rows = c0.shape[0]
    in_width = mine_ref.shape[1] - HD
    for k, part in enumerate((c0, c1, c2, c3)):
        here = slice(k * rows, (k + 1) * rows)
        for out_ref, flips in ((mine_ref, (0,)), (near_ref, (1, 2)), (wrap_ref, (3, 2))):
            out_ref[here, :in_width] = part[:, :in_width]
            for i, j in enumerate(flips):
                at = pl.multiple_of(in_width + (info_ref[X_AT] ^ j) * HD, HD)
                to = in_width + i * HD
                out_ref[here, to : to + HD] = part[:, pl.ds(at, HD)]


def forward_kernel(
    src_ref, x_ref, scale_ref, gains_ref, cos_ref, sin_ref, weights_ref,
    part_ref, normed_ref, raw_ref,
):
    rows = x_ref.shape[0]
    in_width = raw_ref.shape[1]
    total = weights_ref.shape[1]
    normed_ref[...] = input_norm(x_ref[...], scale_ref[...])[2]
    rows_of(normed_ref, weights_ref, src_ref, raw_ref, 0, in_width)
    attn = attend(raw_ref[...], gains_ref[...], cos_ref[...], sin_ref[...], total - in_width)[-1]
    columns_of(side_by_side(attn, rows), weights_ref, src_ref, part_ref, 0, in_width, total)


def post_kernel(
    core_ref, own_ref, other_ref, x_ref, cot_ref, saved_ref, scale_ref,
    out_ref, grad_ref, passed_ref, norm_ref,
):
    rows = x_ref.shape[0]
    sums = own_ref[...].astype(F32) + other_ref[...].astype(F32)
    out = (x_ref[...].astype(F32) + sums[:rows]).astype(BF16)
    inverse, unit, _ = input_norm(saved_ref[...], scale_ref[...])
    d_normed = sums[rows:]
    back = unit_back(d_normed * scale_ref[...], unit, inverse)
    grad = (cot_ref[...].astype(F32) + back).astype(BF16)
    out_ref[...] = out
    grad_ref[...] = grad
    norm_ref[...] = jnp.sum(d_normed * unit, axis=0, keepdims=True)

    @pl.when(core_ref[CORE_AT] == 0)
    def _():
        passed_ref[...] = out

    @pl.when(core_ref[CORE_AT] != 0)
    def _():
        passed_ref[...] = grad


def weights_kernel(
    info_ref, n0, n1, n2, n3, e0, e1, e2, e3, e4, l0, l1, l2, l3, l4,
    query_ref, key_ref, value_ref, out_ref, features_ref, *, scale
):
    rows = n0.shape[0] // SIDE
    q_width = query_ref.shape[2]
    in_width = q_width + 2 * HD
    for i, (j, k) in enumerate(FLIPS):
        for c in range(3):
            features_ref[c, i * rows : (i + 1) * rows, :] = (n0, n1, n2, n3)[k][
                j * rows : (j + 1) * rows, c * HD : (c + 1) * HD
            ]
    grad_in, grad_out, at = 0.0, 0.0, 0
    for i, (early, late) in enumerate(zip((e0, e1, e2, e3, e4), (l0, l1, l2, l3, l4))):
        here = slice(at, at + early.shape[0])
        at += early.shape[0]
        cot_at = in_width + (HD if i > 2 else 0)
        grad_in += dot(features_ref[0, here, :], early[:, :in_width], 0, 0)
        grad_in += dot(features_ref[1, here, :], late[:, :in_width], 0, 0)
        grad_out += dot(features_ref[2, here, :], early[:, in_width : in_width + q_width], 0, 0)
        grad_out += dot(late[:, cot_at : cot_at + HD], early[:, in_width + q_width :], 0, 0)
    query_ref[0] = scale * grad_in[:, :q_width]
    key_ref[0] = scale * grad_in[:, q_width : q_width + HD]
    value_ref[0] = scale * grad_in[:, q_width + HD :]
    out_ref[0] = scale * grad_out


def kernel_call(kernel, out_shape, *operands, scratch=(), aliases=None):
    spec = [pl.BlockSpec(memory_space=pltpu.SMEM)]
    spec += [pl.BlockSpec(memory_space=pltpu.VMEM)] * (len(operands) - 1)
    return pl.pallas_call(
        kernel,
        in_specs=spec,
        out_specs=jax.tree.map(lambda _: pl.BlockSpec(memory_space=pltpu.VMEM), out_shape),
        out_shape=out_shape,
        scratch_shapes=scratch,
        input_output_aliases=aliases or {},
        compiler_params=pltpu.CompilerParams(vmem_limit_bytes=VMEM_LIMIT),
        interpret=INTERPRET,
    )(*operands)


def rope_tables(length, copies):
    half_width = HD // 2
    freqs = jnp.exp(jnp.arange(half_width, dtype=F32) * (-2.0 * math.log(THETA) / HD))
    angles = jnp.arange(length, dtype=F32)[:, None] * freqs[None, :]
    cos_half, sin_half = jnp.cos(angles), jnp.sin(angles)
    cos_tab = jnp.concatenate([cos_half, cos_half], axis=1)
    sin_tab = jnp.concatenate([-sin_half, sin_half], axis=1)
    return jnp.tile(cos_tab, (copies, 1)), jnp.tile(sin_tab, (copies, 1))


def input_norm(rows, norm_scale):
    wide = rows.astype(F32)
    inverse = lax.rsqrt(jnp.mean(wide * wide, axis=-1, keepdims=True) + EPSILON)
    unit = wide * inverse
    return inverse, unit, (unit * norm_scale).astype(BF16)


def local(
    fwd_input,
    fresh_input,
    cotangent,
    fresh_cotangent,
    stash,
    norm_gain,
    qk_gain,
    w_query,
    w_key,
    w_value,
    w_out,
):
    replica = lax.axis_index("dp")
    z, x = replica // SIDE, replica % SIDE
    section = lax.axis_index("section")
    sections = lax.axis_size("section")
    core = lax.axis_index("tensor")
    q_width = w_query.shape[2]
    in_width = q_width + w_key.shape[2] + w_value.shape[2]
    rows = fwd_input.shape[1]
    norm_scale, gains = norm_gain[0], qk_gain[0]
    cos_tab, sin_tab = rope_tables(rows, q_width // HD)
    tables = (gains, cos_tab, sin_tab)

    shard = jnp.concatenate([w_query[0], w_key[0], w_value[0], w_out[0]], axis=1)
    total_width = shard.shape[1]
    pieces, sources = gather_weights(shard, z)
    info = jnp.concatenate([sources, jnp.stack([z, x, core])])
    mirror = [(s, sections - 1 - s) for s in range(sections)]
    fetched = lax.ppermute(jnp.where(core == 0, stash[0, 0], stash[0, 1]), "section", mirror)
    shared = other_core(fetched)
    reloaded = jnp.where(core == 0, fetched, shared), jnp.where(core == 0, shared, fetched)
    features = fwd_input.shape[2]
    width = features // SIDE

    def input_grad(cot_rows, d_normed, unit, inverse):
        back = unit_back(d_normed * norm_scale, unit, inverse)
        return (cot_rows.astype(F32) + back).astype(BF16)

    x_first, cot_first = fwd_input[0], cotangent[0]
    inv_2, unit_2, _ = input_norm(reloaded[1], norm_scale)
    parted = jax.ShapeDtypeStruct((rows, 3 * features // SIDE), BF16)
    normed, *parted = kernel_call(
        prepare_kernel,
        (jax.ShapeDtypeStruct((3 * rows, features), BF16), parted, parted, parted, parted),
        info, *reloaded, x_first, cot_first, norm_gain,
    )
    early = own_features(sent_along_x(parted))
    whole = jax.ShapeDtypeStruct((features, total_width), BF16)
    gate = pieces[2][3]
    first_three = [held_until(piece, gate) for group in pieces[:2] for piece in group[3:]]
    three = kernel_call(
        three_groups_kernel, whole, info,
        *pieces[0][:3], *first_three[:2], *pieces[1][:3], first_three[2], *pieces[2],
    )
    parts, early_block, terms_1, raw_2, weights = kernel_call(
        first_kernel,
        (
            jax.ShapeDtypeStruct((2 * rows, features), BF16),
            jax.ShapeDtypeStruct((rows, in_width + 2 * q_width), BF16),
            jax.ShapeDtypeStruct((2, HD), F32),
            jax.ShapeDtypeStruct((rows, in_width), F32),
            whole,
        ),
        info, normed, cot_first, *tables, *pieces[3], three,
        aliases={10: 4},
        scratch=[pltpu.VMEM((3 * rows, in_width), F32), pltpu.VMEM((rows, q_width), F32)],
    )
    block = jax.ShapeDtypeStruct((rows, features), BF16)
    out_first, grad_first, passed, norm_term_1 = kernel_call(
        post_kernel,
        (block, block, block, jax.ShapeDtypeStruct((1, features), F32)),
        info, parts, other_core(parts),
        x_first, cot_first, reloaded[0], norm_gain,
    )

    onward = [(2 * s, 2 * s + 2) for s in range(sections - 1)]
    back = [(2 * s + 1, 2 * s - 1) for s in range(1, sections)]
    passed = lax.ppermute(passed, ("section", "tensor"), onward + back)
    passed = jnp.where((core == 0) & (section == 0), fresh_input, passed)
    passed = jnp.where((core == 1) & (section == sections - 1), fresh_cotangent, passed)
    swapped = other_core(passed)
    x_second = jnp.where(core == 0, passed, swapped)
    cot_second = jnp.where(core == 0, swapped, passed)

    payload = jax.ShapeDtypeStruct((rows, in_width + width), BF16)
    *payloads, back_part, terms_2 = kernel_call(
        backward_kernel,
        (payload, payload, payload, payload, block, jax.ShapeDtypeStruct((2, HD), F32)),
        info, raw_2, cot_second, *tables, weights,
        scratch=[pltpu.VMEM((rows, q_width), F32)],
    )
    early_rows = gather_rows(early_block, passed)
    out_part = kernel_call(
        forward_kernel,
        block,
        info, x_second, norm_gain, *tables, weights,
        scratch=[pltpu.VMEM((rows, features), BF16), pltpu.VMEM((rows, in_width), F32)],
    )
    parts = lax.optimization_barrier(jnp.concatenate([out_part, back_part], axis=0))
    others = other_core(parts)
    sums = parts.astype(F32) + others.astype(F32)
    out_second = (x_second.astype(F32) + sums[:rows]).astype(BF16)
    d_normed_2 = sums[rows:]
    grad_second = input_grad(cot_second, d_normed_2, unit_2, inv_2)
    flips = [along_dp(payloads[k], z_flip(k)) for k in range(1, SIDE)]
    flips = [held_until(flip, others) for flip in flips]
    onto_x = jax.ShapeDtypeStruct((SIDE * rows, in_width + 2 * HD), BF16)
    mine, to_near, to_wrap = kernel_call(
        spread_kernel,
        (jax.ShapeDtypeStruct((SIDE * rows, in_width + HD), BF16), onto_x, onto_x),
        info, payloads[0], *flips,
    )
    late_rows = mine, *spread_along_x(to_near, to_wrap)

    out_activations = jnp.stack([out_first, out_second])[None]
    grad_input = jnp.stack([grad_first, grad_second])[None]

    scale = 1.0 / math.sqrt(2 * rows * lax.axis_size("dp"))
    like = [jax.ShapeDtypeStruct(w.shape, F32) for w in (w_query, w_key, w_value, w_out)]
    grads = kernel_call(
        functools.partial(weights_kernel, scale=scale),
        tuple(like),
        info, *early, *early_rows, *late_rows,
        scratch=[pltpu.VMEM((3, rows * SIDE * SIDE, HD), BF16)],
    )

    norm_term = norm_term_1[0] + jnp.sum(d_normed_2 * unit_2, axis=0)
    qk_term = terms_1 + terms_2
    qk_term = qk_term + other_core(qk_term)
    total = sum_over_dp(jnp.concatenate([norm_term.reshape(-1, HD), qk_term], axis=0) * scale)
    return (
        out_activations,
        grad_input,
        *grads,
        total[:-2].reshape(1, -1),
        total[-2:][None],
    )


def solution(mesh):
    return jax.shard_map(
        local,
        mesh=mesh,
        in_specs=(
            P("section", "dp", None),
            P("dp", None),
            P("section", "dp", None),
            P("dp", None),
            P("section", None, "dp", None),
            P("section", None),
            P("section", None, None),
            P("section", "dp", "tensor"),
            P("section", "dp", "tensor"),
            P("section", "dp", "tensor"),
            P("section", "dp", "tensor"),
        ),
        out_specs=(
            P("section", None, "dp", None),
            P("section", None, "dp", None),
            P("section", "dp", "tensor"),
            P("section", "dp", "tensor"),
            P("section", "dp", "tensor"),
            P("section", "dp", "tensor"),
            P("section", None),
            P("section", None, None),
        ),
        check_vma=False,
    )
```

```python
import functools
import math

import jax
import jax.numpy as jnp
from jax import lax
from jax.experimental import pallas as pl
from jax.experimental.pallas import tpu as pltpu
from jax.sharding import PartitionSpec as P


HD = 128
EPSILON = 1e-06
THETA = 1000000.0
SIDE = 4
F32 = jnp.float32
BF16 = jnp.bfloat16
INTERPRET = False
Z_AT, X_AT, CORE_AT = 4, 5, 6
VMEM_LIMIT = 10 * 1024 * 1024


LINE_RING = {0: 1, 1: 3, 3: 2, 2: 0}


def z_ring():
    return [(z * SIDE + x, LINE_RING[z] * SIDE + x) for z in range(SIDE) for x in range(SIDE)]


def z_flip(k):
    return [(z * SIDE + x, (z ^ k) * SIDE + x) for z in range(SIDE) for x in range(SIDE)]


def x_flip(k):
    return [(z * SIDE + x, z * SIDE + (x ^ k)) for z in range(SIDE) for x in range(SIDE)]


def along_dp(array, route):
    return lax.ppermute(array, "dp", route)


def other_core(array):
    return lax.ppermute(array, "tensor", [(0, 1), (1, 0)])


def held_until(array, other):
    corner = other[(0,) * (other.ndim - 2)][:16, :HD]
    return lax.optimization_barrier((array, corner))[0]


def gather_weights(shard, z):
    rows = shard.shape[0]
    half = rows // 2
    held = [shard]
    for _ in range(1, SIDE):
        held.append(along_dp(held[-1], z_ring()))
    pieces, sources = [], []
    source = z
    for step, mine in enumerate(held):
        near = along_dp(mine, x_flip(1))
        wrap = along_dp(mine, x_flip(3))
        if step < 2:
            far_top = near[:half]
            far_low = wrap[half:]
            far_top = along_dp(far_top, x_flip(3))
            far_low = along_dp(far_low, x_flip(1))
            across = far_top, far_low
            if step == 1:
                across = (jnp.concatenate(across, axis=0),)
        else:
            across = (along_dp(across[0], z_ring()),)
        pieces.append((mine, near, wrap, *across))
        sources.append(source)
        source = jnp.where(source == 0, 2, jnp.where(source == 1, 0, jnp.where(source == 2, 3, 1)))
    return pieces, jnp.stack(sources)


FLIPS = [(j, k) for j in (0, 1, 3, 2) for k in range(SIDE)]


def gather_rows(block, gate):
    flips = [along_dp(block, z_flip(k)) for k in range(1, SIDE)]
    flips = [held_until(flip, gate) for flip in flips]
    mine = jnp.concatenate([block] + flips, axis=0)
    return mine, *spread_along_x(mine, mine)


def spread_along_x(to_near, to_wrap):
    half = to_near.shape[0] // 2
    near = along_dp(to_near, x_flip(1))
    wrap = along_dp(to_wrap, x_flip(3))
    far_top = along_dp(near[:half], x_flip(3))
    far_low = along_dp(wrap[half:], x_flip(1))
    return near, wrap, far_top, far_low


def sent_along_x(parted):
    flips = [along_dp(parted[j], x_flip(j)) for j in range(1, SIDE)]
    return parted[:1] + flips


def own_features(came):
    width = came[0].shape[1] // SIDE
    stacks = [
        jnp.concatenate([part[:, k * width : (k + 1) * width] for part in came], axis=0)
        for k in range(SIDE)
    ]
    return stacks[:1] + [along_dp(stacks[k], z_flip(k)) for k in range(1, SIDE)]


def sum_over_dp(array):
    for route in (x_flip(1), x_flip(2), z_flip(1), z_flip(2)):
        array = array + along_dp(array, route)
    return array


def stacked(rows_by_columns):
    count = rows_by_columns.shape[1] // HD
    return jnp.concatenate(
        [rows_by_columns[:, i * HD : (i + 1) * HD] for i in range(count)], axis=0
    )


def side_by_side(stack, rows):
    count = stack.shape[0] // rows
    return jnp.concatenate([stack[i * rows : (i + 1) * rows] for i in range(count)], axis=1)


def rope(vectors, cos_tab, sin_tab):
    return vectors * cos_tab + pltpu.roll(vectors, HD // 2, 1) * sin_tab


def unrope(vectors, cos_tab, sin_tab):
    return vectors * cos_tab - pltpu.roll(vectors, HD // 2, 1) * sin_tab


def head_norm(raw):
    inverse = lax.rsqrt(jnp.mean(raw * raw, axis=-1, keepdims=True) + EPSILON)
    return raw * inverse, inverse


def unit_back(grad_unit, unit, inverse):
    return inverse * (grad_unit - unit * jnp.mean(grad_unit * unit, axis=-1, keepdims=True))


def dot(a, b, a_dim, b_dim):
    return lax.dot_general(a, b, (((a_dim,), (b_dim,)), ((), ())), preferred_element_type=F32)


def attend(raw, gains, cos_tab, sin_tab, q_width):
    rows = raw.shape[0]
    q_unit, q_inv = head_norm(stacked(raw[:, :q_width]))
    k_unit, k_inv = head_norm(raw[:, q_width : q_width + HD])
    query = rope(q_unit * gains[0:1], cos_tab, sin_tab).astype(BF16)
    key = rope(k_unit * gains[1:2], cos_tab[:rows], sin_tab[:rows]).astype(BF16)
    value = raw[:, q_width + HD :].astype(BF16)
    scores = dot(query, key, 1, 1) * (1.0 / math.sqrt(HD))
    position = lax.broadcasted_iota(jnp.int32, scores.shape, 0) & (rows - 1)
    causal = position >= lax.broadcasted_iota(jnp.int32, scores.shape, 1)
    raised = jnp.where(causal, jnp.exp(scores), 0.0)
    probs = raised / jnp.sum(raised, axis=-1, keepdims=True)
    probs_b = probs.astype(BF16)
    attn = dot(probs_b, value, 1, 0).astype(BF16)
    return q_unit, q_inv, k_unit, k_inv, query, key, value, probs, probs_b, attn


def columns_of(activations, weights_ref, src_ref, out_ref, top, first, last):
    rows = activations.shape[0]
    width = out_ref.shape[1] // SIDE

    def group(i, carry):
        at = pl.multiple_of(src_ref[i] * width, width)
        here = pl.ds(pl.multiple_of(i * width, width), width)
        product = dot(activations, weights_ref[here, first:last], 1, 1).astype(BF16)
        out_ref[top : top + rows, pl.ds(at, width)] = product
        return carry

    lax.fori_loop(0, SIDE, group, 0)


def rows_of(rows_ref, weights_ref, src_ref, sum_ref, first, last, groups):
    width = rows_ref.shape[1] // SIDE

    def group(i, carry):
        at = pl.multiple_of(src_ref[i] * width, width)
        here = pl.ds(pl.multiple_of(i * width, width), width)
        sum_ref[...] += dot(rows_ref[:, pl.ds(at, width)], weights_ref[here, first:last], 1, 0)
        return carry

    lax.fori_loop(*groups, group, 0)


def back_attention(raw, d_attn, gains, cos_tab, sin_tab, terms_ref):
    rows = raw.shape[0]
    q_unit, q_inv, k_unit, k_inv, query, key, value, probs, probs_b, attn = attend(
        raw, gains, cos_tab, sin_tab, d_attn.shape[1]
    )
    d_attn = stacked(d_attn)
    d_probs = dot(d_attn, value, 1, 1)
    d_value = dot(probs_b, d_attn, 0, 0).astype(BF16)
    d_scores = (
        probs
        * (d_probs - jnp.sum(probs * d_probs, axis=-1, keepdims=True))
        * (1.0 / math.sqrt(HD))
    ).astype(BF16)
    dq_r = unrope(dot(d_scores, key, 1, 0), cos_tab, sin_tab)
    dk_r = unrope(dot(d_scores, query, 0, 0), cos_tab[:rows], sin_tab[:rows])
    terms_ref[0:1, :] = jnp.sum(dq_r * q_unit, axis=0, keepdims=True)
    terms_ref[1:2, :] = jnp.sum(dk_r * k_unit, axis=0, keepdims=True)
    q_grad = unit_back(dq_r * gains[0:1], q_unit, q_inv).astype(BF16)
    k_grad = unit_back(dk_r * gains[1:2], k_unit, k_inv).astype(BF16)
    columns = jnp.concatenate([side_by_side(q_grad, rows), k_grad, d_value], axis=1)
    return side_by_side(attn, rows), columns


TILE = 16


def put_group(step, pieces, src_ref, weights_ref):
    size = pieces[0].shape[0]
    places = [(0, 0), (1, 0), (3, 0), (2, 0), (2, pieces[3].shape[0])]
    for piece, (flip, down) in zip(pieces, places):
        top = (step * SIDE + (src_ref[X_AT] ^ flip)) * size + down

        def put(i, carry, piece=piece, top=top):
            here = pl.multiple_of(i * TILE, TILE)
            there = pl.multiple_of(top + i * TILE, TILE)
            weights_ref[pl.ds(there, TILE), :] = piece[pl.ds(here, TILE), :]
            return carry

        lax.fori_loop(0, piece.shape[0] // TILE, put, 0)


def three_groups_kernel(src_ref, normed_ref, cot_ref, *refs):
    *pieces, weights_ref, raw_ref, d_attn_ref = refs
    put_group(0, pieces[:5], src_ref, weights_ref)
    put_group(1, pieces[5:9], src_ref, weights_ref)
    put_group(2, pieces[9:13], src_ref, weights_ref)
    in_width, total = raw_ref.shape[1], weights_ref.shape[1]
    raw_ref[...] = jnp.zeros(raw_ref.shape, F32)
    d_attn_ref[...] = jnp.zeros(d_attn_ref.shape, F32)
    rows_of(normed_ref, weights_ref, src_ref, raw_ref, 0, in_width, (0, 3))
    rows_of(cot_ref, weights_ref, src_ref, d_attn_ref, in_width, total, (0, 3))


def first_kernel(
    src_ref, normed_ref, cot_ref, gains_ref, cos_ref, sin_ref, raw_3_ref, d_attn_3_ref,
    s0, s1, s2, s3, three_ref,
    parts_ref, early_ref, terms_ref, raw_2_ref, weights_ref, raw_ref, d_attn_ref,
):
    put_group(3, (s0, s1, s2, s3), src_ref, weights_ref)
    rows, q_width = d_attn_ref.shape
    in_width = raw_ref.shape[1]
    total = weights_ref.shape[1]
    raw_ref[...] = raw_3_ref[...]
    d_attn_ref[...] = d_attn_3_ref[...]
    rows_of(normed_ref, weights_ref, src_ref, raw_ref, 0, in_width, (3, 4))
    rows_of(cot_ref, weights_ref, src_ref, d_attn_ref, in_width, total, (3, 4))
    raw_2_ref[...] = raw_ref[2 * rows :, :]
    tables = (gains_ref[...], cos_ref[...], sin_ref[...])
    attn_1, columns = back_attention(
        raw_ref[:rows, :], d_attn_ref[...].astype(BF16), *tables, terms_ref
    )
    attn_f = side_by_side(attend(raw_ref[rows : 2 * rows, :], *tables, q_width)[-1], rows)
    attn_2 = side_by_side(attend(raw_ref[2 * rows :, :], *tables, q_width)[-1], rows)
    early_ref[:, :in_width] = columns
    early_ref[:, in_width : in_width + q_width] = attn_1
    early_ref[:, in_width + q_width :] = attn_2
    columns_of(attn_f, weights_ref, src_ref, parts_ref, 0, in_width, total)
    columns_of(columns, weights_ref, src_ref, parts_ref, rows, 0, in_width)


def prepare_kernel(
    info_ref, first_ref, second_ref, x_ref, cot_ref, scale_ref, normed_ref, p0, p1, p2, p3
):
    rows, features = cot_ref.shape
    for i, saved in enumerate((first_ref, x_ref, second_ref)):
        normed_ref[i * rows : (i + 1) * rows, :] = input_norm(saved[...], scale_ref[...])[2]
    width = features // (SIDE * SIDE)
    for j, part in enumerate((p0, p1, p2, p3)):
        for k in range(SIDE):
            replica = (info_ref[Z_AT] ^ k) * SIDE + (info_ref[X_AT] ^ j)
            here = pl.ds(pl.multiple_of(replica * width, width), width)
            at = 3 * k * width
            part[:, at : at + width] = normed_ref[0:rows, here]
            part[:, at + width : at + 2 * width] = normed_ref[2 * rows : 3 * rows, here]
            part[:, at + 2 * width : at + 3 * width] = cot_ref[:, here]


def backward_kernel(
    src_ref, raw_ref, cot_ref, gains_ref, cos_ref, sin_ref, weights_ref,
    c0, c1, c2, c3, part_ref, terms_ref, d_attn_ref,
):
    features = cot_ref.shape[1]
    in_width = raw_ref.shape[1]
    d_attn_ref[...] = jnp.zeros(d_attn_ref.shape, F32)
    rows_of(cot_ref, weights_ref, src_ref, d_attn_ref, in_width, weights_ref.shape[1], (0, SIDE))
    columns = back_attention(
        raw_ref[...], d_attn_ref[...].astype(BF16), gains_ref[...], cos_ref[...], sin_ref[...],
        terms_ref,
    )[1]
    width = features // SIDE
    for k, payload in enumerate((c0, c1, c2, c3)):
        payload[:, :in_width] = columns
        at = pl.multiple_of((src_ref[Z_AT] ^ k) * width, width)
        payload[:, in_width:] = cot_ref[:, pl.ds(at, width)]
    columns_of(columns, weights_ref, src_ref, part_ref, 0, 0, in_width)


def spread_kernel(info_ref, c0, c1, c2, c3, mine_ref, near_ref, wrap_ref):
    rows = c0.shape[0]
    in_width = mine_ref.shape[1] - HD
    for k, part in enumerate((c0, c1, c2, c3)):
        here = slice(k * rows, (k + 1) * rows)
        for out_ref, flips in ((mine_ref, (0,)), (near_ref, (1, 2)), (wrap_ref, (3, 2))):
            out_ref[here, :in_width] = part[:, :in_width]
            for i, j in enumerate(flips):
                at = pl.multiple_of(in_width + (info_ref[X_AT] ^ j) * HD, HD)
                to = in_width + i * HD
                out_ref[here, to : to + HD] = part[:, pl.ds(at, HD)]


def forward_kernel(
    src_ref, x_ref, scale_ref, gains_ref, cos_ref, sin_ref, weights_ref,
    part_ref, normed_ref, raw_ref,
):
    rows = x_ref.shape[0]
    in_width = raw_ref.shape[1]
    total = weights_ref.shape[1]
    normed_ref[...] = input_norm(x_ref[...], scale_ref[...])[2]
    raw_ref[...] = jnp.zeros(raw_ref.shape, F32)
    rows_of(normed_ref, weights_ref, src_ref, raw_ref, 0, in_width, (0, SIDE))
    attn = attend(raw_ref[...], gains_ref[...], cos_ref[...], sin_ref[...], total - in_width)[-1]
    columns_of(side_by_side(attn, rows), weights_ref, src_ref, part_ref, 0, in_width, total)


def post_kernel(
    core_ref, own_ref, other_ref, x_ref, cot_ref, saved_ref, scale_ref,
    out_ref, grad_ref, passed_ref, norm_ref,
):
    rows = x_ref.shape[0]
    sums = own_ref[...].astype(F32) + other_ref[...].astype(F32)
    out = (x_ref[...].astype(F32) + sums[:rows]).astype(BF16)
    inverse, unit, _ = input_norm(saved_ref[...], scale_ref[...])
    d_normed = sums[rows:]
    back = unit_back(d_normed * scale_ref[...], unit, inverse)
    grad = (cot_ref[...].astype(F32) + back).astype(BF16)
    out_ref[...] = out
    grad_ref[...] = grad
    norm_ref[...] = jnp.sum(d_normed * unit, axis=0, keepdims=True)

    @pl.when(core_ref[CORE_AT] == 0)
    def _():
        passed_ref[...] = out

    @pl.when(core_ref[CORE_AT] != 0)
    def _():
        passed_ref[...] = grad


def weights_kernel(
    info_ref, n0, n1, n2, n3, e0, e1, e2, e3, e4, l0, l1, l2, l3, l4,
    query_ref, key_ref, value_ref, out_ref, features_ref, *, scale
):
    rows = n0.shape[0] // SIDE
    q_width = query_ref.shape[2]
    in_width = q_width + 2 * HD
    for i, (j, k) in enumerate(FLIPS):
        for c in range(3):
            features_ref[c, i * rows : (i + 1) * rows, :] = (n0, n1, n2, n3)[k][
                j * rows : (j + 1) * rows, c * HD : (c + 1) * HD
            ]
    grad_in, grad_out, at = 0.0, 0.0, 0
    for i, (early, late) in enumerate(zip((e0, e1, e2, e3, e4), (l0, l1, l2, l3, l4))):
        here = slice(at, at + early.shape[0])
        at += early.shape[0]
        cot_at = in_width + (HD if i > 2 else 0)
        grad_in += dot(features_ref[0, here, :], early[:, :in_width], 0, 0)
        grad_in += dot(features_ref[1, here, :], late[:, :in_width], 0, 0)
        grad_out += dot(features_ref[2, here, :], early[:, in_width : in_width + q_width], 0, 0)
        grad_out += dot(late[:, cot_at : cot_at + HD], early[:, in_width + q_width :], 0, 0)
    query_ref[0] = scale * grad_in[:, :q_width]
    key_ref[0] = scale * grad_in[:, q_width : q_width + HD]
    value_ref[0] = scale * grad_in[:, q_width + HD :]
    out_ref[0] = scale * grad_out


def kernel_call(kernel, out_shape, *operands, scratch=(), aliases=None):
    spec = [pl.BlockSpec(memory_space=pltpu.SMEM)]
    spec += [pl.BlockSpec(memory_space=pltpu.VMEM)] * (len(operands) - 1)
    return pl.pallas_call(
        kernel,
        in_specs=spec,
        out_specs=jax.tree.map(lambda _: pl.BlockSpec(memory_space=pltpu.VMEM), out_shape),
        out_shape=out_shape,
        scratch_shapes=scratch,
        input_output_aliases=aliases or {},
        compiler_params=pltpu.CompilerParams(vmem_limit_bytes=VMEM_LIMIT),
        interpret=INTERPRET,
    )(*operands)


def rope_tables(length, copies):
    half_width = HD // 2
    freqs = jnp.exp(jnp.arange(half_width, dtype=F32) * (-2.0 * math.log(THETA) / HD))
    angles = jnp.arange(length, dtype=F32)[:, None] * freqs[None, :]
    cos_half, sin_half = jnp.cos(angles), jnp.sin(angles)
    cos_tab = jnp.concatenate([cos_half, cos_half], axis=1)
    sin_tab = jnp.concatenate([-sin_half, sin_half], axis=1)
    return jnp.tile(cos_tab, (copies, 1)), jnp.tile(sin_tab, (copies, 1))


def input_norm(rows, norm_scale):
    wide = rows.astype(F32)
    inverse = lax.rsqrt(jnp.mean(wide * wide, axis=-1, keepdims=True) + EPSILON)
    unit = wide * inverse
    return inverse, unit, (unit * norm_scale).astype(BF16)


def local(
    fwd_input,
    fresh_input,
    cotangent,
    fresh_cotangent,
    stash,
    norm_gain,
    qk_gain,
    w_query,
    w_key,
    w_value,
    w_out,
):
    replica = lax.axis_index("dp")
    z, x = replica // SIDE, replica % SIDE
    section = lax.axis_index("section")
    sections = lax.axis_size("section")
    core = lax.axis_index("tensor")
    q_width = w_query.shape[2]
    in_width = q_width + w_key.shape[2] + w_value.shape[2]
    rows = fwd_input.shape[1]
    norm_scale, gains = norm_gain[0], qk_gain[0]
    cos_tab, sin_tab = rope_tables(rows, q_width // HD)
    tables = (gains, cos_tab, sin_tab)

    shard = jnp.concatenate([w_query[0], w_key[0], w_value[0], w_out[0]], axis=1)
    total_width = shard.shape[1]
    pieces, sources = gather_weights(shard, z)
    info = jnp.concatenate([sources, jnp.stack([z, x, core])])
    mirror = [(s, sections - 1 - s) for s in range(sections)]
    fetched = lax.ppermute(jnp.where(core == 0, stash[0, 0], stash[0, 1]), "section", mirror)
    shared = other_core(fetched)
    reloaded = jnp.where(core == 0, fetched, shared), jnp.where(core == 0, shared, fetched)
    features = fwd_input.shape[2]
    width = features // SIDE

    def input_grad(cot_rows, d_normed, unit, inverse):
        back = unit_back(d_normed * norm_scale, unit, inverse)
        return (cot_rows.astype(F32) + back).astype(BF16)

    x_first, cot_first = fwd_input[0], cotangent[0]
    inv_2, unit_2, _ = input_norm(reloaded[1], norm_scale)
    parted = jax.ShapeDtypeStruct((rows, 3 * features // SIDE), BF16)
    normed, *parted = kernel_call(
        prepare_kernel,
        (jax.ShapeDtypeStruct((3 * rows, features), BF16), parted, parted, parted, parted),
        info, *reloaded, x_first, cot_first, norm_gain,
    )
    early = own_features(sent_along_x(parted))
    whole = jax.ShapeDtypeStruct((features, total_width), BF16)
    gate = pieces[2][3]
    first_three = [held_until(piece, gate) for group in pieces[:2] for piece in group[3:]]
    three, raw_3, d_attn_3 = kernel_call(
        three_groups_kernel,
        (
            whole,
            jax.ShapeDtypeStruct((3 * rows, in_width), F32),
            jax.ShapeDtypeStruct((rows, q_width), F32),
        ),
        info, normed, cot_first,
        *pieces[0][:3], *first_three[:2], *pieces[1][:3], first_three[2], *pieces[2],
    )
    parts, early_block, terms_1, raw_2, weights = kernel_call(
        first_kernel,
        (
            jax.ShapeDtypeStruct((2 * rows, features), BF16),
            jax.ShapeDtypeStruct((rows, in_width + 2 * q_width), BF16),
            jax.ShapeDtypeStruct((2, HD), F32),
            jax.ShapeDtypeStruct((rows, in_width), F32),
            whole,
        ),
        info, normed, cot_first, *tables, raw_3, d_attn_3, *pieces[3], three,
        aliases={12: 4},
        scratch=[pltpu.VMEM((3 * rows, in_width), F32), pltpu.VMEM((rows, q_width), F32)],
    )
    block = jax.ShapeDtypeStruct((rows, features), BF16)
    out_first, grad_first, passed, norm_term_1 = kernel_call(
        post_kernel,
        (block, block, block, jax.ShapeDtypeStruct((1, features), F32)),
        info, parts, other_core(parts),
        x_first, cot_first, reloaded[0], norm_gain,
    )

    onward = [(2 * s, 2 * s + 2) for s in range(sections - 1)]
    back = [(2 * s + 1, 2 * s - 1) for s in range(1, sections)]
    passed = lax.ppermute(passed, ("section", "tensor"), onward + back)
    passed = jnp.where((core == 0) & (section == 0), fresh_input, passed)
    passed = jnp.where((core == 1) & (section == sections - 1), fresh_cotangent, passed)
    swapped = other_core(passed)
    x_second = jnp.where(core == 0, passed, swapped)
    cot_second = jnp.where(core == 0, swapped, passed)

    payload = jax.ShapeDtypeStruct((rows, in_width + width), BF16)
    *payloads, back_part, terms_2 = kernel_call(
        backward_kernel,
        (payload, payload, payload, payload, block, jax.ShapeDtypeStruct((2, HD), F32)),
        info, raw_2, cot_second, *tables, weights,
        scratch=[pltpu.VMEM((rows, q_width), F32)],
    )
    early_rows = gather_rows(early_block, passed)
    out_part = kernel_call(
        forward_kernel,
        block,
        info, x_second, norm_gain, *tables, weights,
        scratch=[pltpu.VMEM((rows, features), BF16), pltpu.VMEM((rows, in_width), F32)],
    )
    parts = lax.optimization_barrier(jnp.concatenate([out_part, back_part], axis=0))
    others = other_core(parts)
    sums = parts.astype(F32) + others.astype(F32)
    out_second = (x_second.astype(F32) + sums[:rows]).astype(BF16)
    d_normed_2 = sums[rows:]
    grad_second = input_grad(cot_second, d_normed_2, unit_2, inv_2)
    flips = [along_dp(payloads[k], z_flip(k)) for k in range(1, SIDE)]
    flips = [held_until(flip, others) for flip in flips]
    onto_x = jax.ShapeDtypeStruct((SIDE * rows, in_width + 2 * HD), BF16)
    mine, to_near, to_wrap = kernel_call(
        spread_kernel,
        (jax.ShapeDtypeStruct((SIDE * rows, in_width + HD), BF16), onto_x, onto_x),
        info, payloads[0], *flips,
    )
    late_rows = mine, *spread_along_x(to_near, to_wrap)

    out_activations = jnp.stack([out_first, out_second])[None]
    grad_input = jnp.stack([grad_first, grad_second])[None]

    scale = 1.0 / math.sqrt(2 * rows * lax.axis_size("dp"))
    like = [jax.ShapeDtypeStruct(w.shape, F32) for w in (w_query, w_key, w_value, w_out)]
    grads = kernel_call(
        functools.partial(weights_kernel, scale=scale),
        tuple(like),
        info, *early, *early_rows, *late_rows,
        scratch=[pltpu.VMEM((3, rows * SIDE * SIDE, HD), BF16)],
    )

    norm_term = norm_term_1[0] + jnp.sum(d_normed_2 * unit_2, axis=0)
    qk_term = terms_1 + terms_2
    qk_term = qk_term + other_core(qk_term)
    total = sum_over_dp(jnp.concatenate([norm_term.reshape(-1, HD), qk_term], axis=0) * scale)
    return (
        out_activations,
        grad_input,
        *grads,
        total[:-2].reshape(1, -1),
        total[-2:][None],
    )


def solution(mesh):
    return jax.shard_map(
        local,
        mesh=mesh,
        in_specs=(
            P("section", "dp", None),
            P("dp", None),
            P("section", "dp", None),
            P("dp", None),
            P("section", None, "dp", None),
            P("section", None),
            P("section", None, None),
            P("section", "dp", "tensor"),
            P("section", "dp", "tensor"),
            P("section", "dp", "tensor"),
            P("section", "dp", "tensor"),
        ),
        out_specs=(
            P("section", None, "dp", None),
            P("section", None, "dp", None),
            P("section", "dp", "tensor"),
            P("section", "dp", "tensor"),
            P("section", "dp", "tensor"),
            P("section", "dp", "tensor"),
            P("section", None),
            P("section", None, None),
        ),
        check_vma=False,
    )
```
